32 devices in a mesh: parts: 2 (over x), mesh: 16 (over z, y, core).
Axes of the slice: x: 2, y: 2, z: 4, core: 2. Of those that a mesh axis runs over, the one named last changes fastest.
Arguments:
- grid_in: bfloat16 [474, 8192], P(None, ('parts', 'mesh')), parts along dimension 1, may hold values from -6 to 6
- mesh_init: bfloat16 [512, 512], P(('parts', 'mesh')), parts along dimension 0, may hold values from -6 to 6
- embed_weight: bfloat16 [474, 512], replicated, may hold values from -0.25 to 0.25
- enc_send: bfloat16 [512, 512], replicated, may hold values from -0.25 to 0.25
- enc_recv: bfloat16 [512, 512], replicated, may hold values from -0.25 to 0.25
- enc_node: bfloat16 [512, 512], replicated, may hold values from -0.25 to 0.25
- mid_send: bfloat16 [512, 512], replicated, may hold values from -0.25 to 0.25
- mid_recv: bfloat16 [512, 512], replicated, may hold values from -0.25 to 0.25
- mid_node: bfloat16 [512, 512], replicated, may hold values from -0.25 to 0.25
- dec_send: bfloat16 [512, 512], replicated, may hold values from -0.25 to 0.25
- dec_recv: bfloat16 [512, 512], replicated, may hold values from -0.25 to 0.25
- dec_node: bfloat16 [512, 512], replicated, may hold values from -0.25 to 0.25
- mid_gain: float32 [512], replicated, may hold values from 0.5 to 1.5
- cotangent: bfloat16 [8192, 512], P(('parts', 'mesh')), parts along dimension 0, may hold values from -0.035888672 to 0.035888672
- enc_from: int32 [48, 256], P('mesh'), may hold values from 0 to 255
- enc_into: int32 [48, 256], P('mesh'), may hold values from 0 to 15
- enc_count: int32 [48], P('mesh'), may hold values from 1 to 256, as said below
- mid_from: int32 [256, 32], P('mesh'), may hold values from 0 to 15
- mid_into: int32 [256, 32], P('mesh'), may hold values from 0 to 15
- mid_count: int32 [256], P('mesh'), may hold values from 0 to 32, as said below
- dec_from: int32 [48, 512], P('mesh'), may hold values from 0 to 15
- dec_into: int32 [48, 512], P('mesh'), may hold values from 0 to 255
- dec_count: int32 [48], P('mesh'), may hold values from 1 to 512, as said below
Outputs:
- update: bfloat16 [8192, 512], P(('parts', 'mesh')), parts along dimension 0
- embed_grad: float32 [948, 512], P('parts'), parts along dimension 0
- encode_grad: float32 [1024, 512], P('parts'), parts along dimension 0
- process_grad: float32 [1024, 512], P('parts'), parts along dimension 0
- decode_grad: float32 [1024, 512], P('parts'), parts along dimension 0
- output_grad: float32 [1024, 512], P('parts'), parts along dimension 0
The draws below stay inside these ranges and needn't reach their ends.
There are 2 independent parts, one for each index of `parts`. The reference program is written for one: setup_inputs(seed, part) draws one part's arguments, and reference() takes and returns one part's arrays. A program takes and returns all parts, laid end to end along the dimension named above; an argument that names none is the same for every part. Nothing has to cross between parts.
Inputs may be any that keep to these rules, and one draw needn't show every extreme that they name: `enc_count`: at most 256; in every draw one destination block is full from each of its 3 neighbouring source blocks. `mid_count`: at most 32; in every draw one destination block is full from every source block. `dec_count`: at most 512; in every draw one destination block is full from each of its 3 neighbouring source blocks.
All inputs are finite; a program needn't handle non-finite values.
Results may differ from the reference program's by a relative error of at most 0.018.
Values may be sent and summed in bfloat16 or wider, within the bound.
A program may use at most 64 MiB of HBM per device.

```python
import jax
import jax.numpy as jnp
from jax import lax

D = 512
CH = 474
SPAN = 3
GRID_DEV = 256
MESH_DEV = 16
CAP_ENC = 256
CAP_DEC = 512
BLOCKS = 16
PAIRS = 256
NEAR = 48
CAP_MID = 32
GRID = 4096
MESH = 256


def skewed_counts(key, cap, columns, lowest):
    keys = jax.random.split(key, 4)
    light = jax.random.randint(keys[0], (BLOCKS, columns), lowest, cap // 2 + 1)
    heavy = cap - jax.random.randint(keys[1], (BLOCKS, columns), 0, cap // 4 + 1)
    busy = jax.random.randint(keys[2], (BLOCKS, 1), 0, 4) == 0
    counts = jnp.where(busy, heavy, light)
    chosen = jax.random.randint(keys[3], (), 0, BLOCKS)
    places = lax.broadcasted_iota(jnp.int32, (BLOCKS, columns), 0)
    counts = jnp.where(places == chosen, cap, counts)
    return counts.reshape(-1).astype(jnp.int32)


def draw_enc_count(key, part):
    return skewed_counts(jax.random.fold_in(key, 101), CAP_ENC, SPAN, 1)


def draw_mid_count(key, part):
    return skewed_counts(jax.random.fold_in(key, 202), CAP_MID, BLOCKS, 0)


def draw_dec_count(key, part):
    return skewed_counts(jax.random.fold_in(key, 303), CAP_DEC, SPAN, 1)


def touch_ends(values, own_key, low, high):
    longest = values.shape.index(max(values.shape))
    spots = []
    for shift in (0, 1):
        where = [jax.random.randint(jax.random.fold_in(own_key, axis), (), 0, length) for axis, length in enumerate(values.shape)]
        where[longest] = (where[longest] + shift) % values.shape[longest]
        spots.append(tuple(where))
    return values.at[spots[0]].set(low).at[spots[1]].set(high)


def block_levels(key, dims, cuts, least, top_value):
    def one(dim, shards_of):
        steps = jax.random.uniform(jax.random.fold_in(jax.random.fold_in(key, 6), dim), (shards_of,), jnp.float32, least / len(cuts), top_value / len(cuts))
        return jnp.repeat(jnp.exp(steps), dims[dim] // shards_of).reshape((-1,) + (1,) * (len(dims) - dim - 1))

    gain = one(*cuts[0])
    for cut in cuts[1:]:
        gain = gain * one(*cut)
    return gain


def scatter_about(stream_key, dims, scale, bound, shards=(), held_as=jnp.bfloat16):
    drawn = jax.random.normal(stream_key, dims, jnp.float32) * scale
    if len(shards) > 0:
        drawn = block_levels(stream_key, dims, shards, -0.22, 0.18) * drawn
    return jnp.clip(drawn, min=-bound, max=bound).astype(held_as)


def setup_inputs(seed: int = 0, part: int = 0) -> dict:
    seeds = jax.random.split(jax.random.key(seed), 24)
    part_keys = jax.random.split(jax.random.fold_in(seeds[23], part), 24)
    grid_in = scatter_about(part_keys[0], (CH, GRID), 1.0, 6.0, ((1, 16),))
    mesh_init = scatter_about(part_keys[1], (MESH, D), 1.0, 6.0, ((0, 16),))
    embed_weight = scatter_about(seeds[2], (CH, D), CH ** -0.5, 0.25)
    enc_send = scatter_about(seeds[3], (D, D), D ** -0.5, 0.25)
    enc_recv = scatter_about(seeds[4], (D, D), D ** -0.5, 0.25)
    enc_node = scatter_about(seeds[5], (D, D), D ** -0.5, 0.25)
    mid_send = scatter_about(seeds[6], (D, D), D ** -0.5, 0.25)
    mid_recv = scatter_about(seeds[7], (D, D), D ** -0.5, 0.25)
    mid_node = scatter_about(seeds[8], (D, D), D ** -0.5, 0.25)
    dec_send = scatter_about(seeds[9], (D, D), D ** -0.5, 0.25)
    dec_recv = scatter_about(seeds[10], (D, D), D ** -0.5, 0.25)
    dec_node = scatter_about(seeds[11], (D, D), D ** -0.5, 0.25)
    mid_gain = jnp.clip(jax.random.uniform(seeds[12], (D,), jnp.float32, 0.5, 1.5), 0.5, 1.5)
    cotangent = scatter_about(part_keys[13], (GRID, D), 0.006, 0.035888672, ((0, 16),))
    enc_from = touch_ends(jax.random.randint(seeds[14], (NEAR, CAP_ENC), 0, GRID_DEV), jax.random.fold_in(seeds[14], 1), 0, GRID_DEV - 1).astype(jnp.int32)
    enc_into = touch_ends(jax.random.randint(seeds[15], (NEAR, CAP_ENC), 0, MESH_DEV), jax.random.fold_in(seeds[15], 1), 0, MESH_DEV - 1).astype(jnp.int32)
    enc_count = draw_enc_count(jax.random.fold_in(seeds[23], 71), part)
    mid_from = touch_ends(jax.random.randint(seeds[17], (PAIRS, CAP_MID), 0, MESH_DEV), jax.random.fold_in(seeds[17], 1), 0, MESH_DEV - 1).astype(jnp.int32)
    mid_into = touch_ends(jax.random.randint(seeds[18], (PAIRS, CAP_MID), 0, MESH_DEV), jax.random.fold_in(seeds[18], 1), 0, MESH_DEV - 1).astype(jnp.int32)
    mid_count = draw_mid_count(jax.random.fold_in(seeds[23], 71), part)
    dec_from = touch_ends(jax.random.randint(seeds[20], (NEAR, CAP_DEC), 0, MESH_DEV), jax.random.fold_in(seeds[20], 1), 0, MESH_DEV - 1).astype(jnp.int32)
    dec_into = touch_ends(jax.random.randint(seeds[21], (NEAR, CAP_DEC), 0, GRID_DEV), jax.random.fold_in(seeds[21], 1), 0, GRID_DEV - 1).astype(jnp.int32)
    dec_count = draw_dec_count(jax.random.fold_in(seeds[23], 71), part)
    return dict(grid_in=grid_in, mesh_init=mesh_init, embed_weight=embed_weight, enc_send=enc_send, enc_recv=enc_recv, enc_node=enc_node, mid_send=mid_send, mid_recv=mid_recv, mid_node=mid_node, dec_send=dec_send, dec_recv=dec_recv, dec_node=dec_node, mid_gain=mid_gain, cotangent=cotangent, enc_from=enc_from, enc_into=enc_into, enc_count=enc_count, mid_from=mid_from, mid_into=mid_into, mid_count=mid_count, dec_from=dec_from, dec_into=dec_into, dec_count=dec_count)


EPSILON = 1e-05

def layer_norm(values):
    center = values - lax.optimization_barrier(jnp.mean(values, axis=-1, keepdims=True))
    spread = lax.optimization_barrier(jnp.mean(center * center, axis=-1, keepdims=True))
    return center * lax.rsqrt(spread + EPSILON)

def silu_slope(values):
    sigma = jax.nn.sigmoid(values)
    return sigma * (1.0 + values * (1.0 - sigma))

def live_slots(count, cap):
    return jnp.arange(cap, dtype=jnp.int32)[None, None, :] < count.reshape(BLOCKS, -1)[:, :, None]

def aggregate(sender, target, source_idx, local_idx, alive, rows):
    width = sender.shape[1]

    def block(pieces):
        from_rows, into_rows, valid, which = pieces
        targets = lax.dynamic_slice_in_dim(target, which * rows, rows, 0)
        inputs = sender[from_rows].astype(jnp.float32) + targets[into_rows].astype(jnp.float32)
        message = jax.nn.silu(inputs).astype(jnp.bfloat16)
        message = lax.optimization_barrier(message).astype(jnp.float32)
        message = jnp.where(valid[..., None], message, 0.0)
        return jax.ops.segment_sum(message.reshape(-1, width), into_rows.reshape(-1), num_segments=rows)
    blocks = jnp.arange(BLOCKS, dtype=jnp.int32)
    return lax.map(block, (source_idx, local_idx, alive, blocks)).reshape(-1, width)

def edge_back(sender, target, source_idx, local_idx, alive, rows, grad_agg):
    width = sender.shape[1]

    def block(carry, pieces):
        from_rows, into_rows, valid, which = pieces
        targets = lax.dynamic_slice_in_dim(target, which * rows, rows, 0)
        grads = lax.dynamic_slice_in_dim(grad_agg, which * rows, rows, 0)
        inputs = sender[from_rows].astype(jnp.float32) + targets[into_rows].astype(jnp.float32)
        grad_in = jnp.where(valid[..., None], grads[into_rows].astype(jnp.float32) * silu_slope(inputs), 0.0)
        grad_in = lax.optimization_barrier(grad_in.astype(jnp.bfloat16)).astype(jnp.float32)
        flat = grad_in.reshape(-1, width)
        carry = carry.at[from_rows.reshape(-1)].add(flat)
        grad_dst = jax.ops.segment_sum(flat, into_rows.reshape(-1), num_segments=rows)
        return (carry, grad_dst)
    blocks = jnp.arange(BLOCKS, dtype=jnp.int32)
    start = jnp.zeros((sender.shape[0], width), jnp.float32)
    total, parts = lax.scan(block, start, (source_idx, local_idx, alive, blocks))
    return (total, parts.reshape(-1, width))

def mm(left, right):
    return jnp.dot(left, right, preferred_element_type=jnp.float32)

def reference(grid_in, mesh_init, embed_weight, enc_send, enc_recv, enc_node, mid_send, mid_recv, mid_node, dec_send, dec_recv, dec_node, mid_gain, cotangent, enc_from, enc_into, enc_count, mid_from, mid_into, mid_count, dec_from, dec_into, dec_count):
    blocks = jnp.arange(BLOCKS, dtype=jnp.int32)
    neighbours = ((blocks[:, None] + jnp.arange(SPAN, dtype=jnp.int32)[None, :] + (BLOCKS - 1)) % BLOCKS).astype(jnp.int32)
    enc_src = (enc_from.reshape(BLOCKS, SPAN, CAP_ENC) + neighbours[:, :, None] * GRID_DEV).astype(jnp.int32)
    enc_dst = enc_into.reshape(BLOCKS, SPAN, CAP_ENC)
    enc_live = live_slots(enc_count, CAP_ENC)
    mid_src = (mid_from.reshape(BLOCKS, BLOCKS, CAP_MID) + blocks[None, :, None] * MESH_DEV).astype(jnp.int32)
    mid_dst = mid_into.reshape(BLOCKS, BLOCKS, CAP_MID)
    mid_live = live_slots(mid_count, CAP_MID)
    dec_src = (dec_from.reshape(BLOCKS, SPAN, CAP_DEC) + neighbours[:, :, None] * MESH_DEV).astype(jnp.int32)
    dec_dst = dec_into.reshape(BLOCKS, SPAN, CAP_DEC)
    dec_live = live_slots(dec_count, CAP_DEC)
    pre_act = mm(grid_in.T, embed_weight)
    hidden = jax.nn.silu(pre_act).astype(jnp.bfloat16)
    enc_proj = mm(hidden, enc_send).astype(jnp.bfloat16)
    enc_target = mm(mesh_init, enc_recv).astype(jnp.bfloat16)
    enc_agg = aggregate(enc_proj, enc_target, enc_src, enc_dst, enc_live, MESH_DEV)
    enc_norm = layer_norm(enc_agg).astype(jnp.bfloat16)
    latent = (mesh_init.astype(jnp.float32) + mm(enc_norm, enc_node)).astype(jnp.bfloat16)
    mid_proj = mm(latent, mid_send).astype(jnp.bfloat16)
    mid_target = mm(latent, mid_recv).astype(jnp.bfloat16)
    mid_agg = aggregate(mid_proj, mid_target, mid_src, mid_dst, mid_live, MESH_DEV)
    mid_norm = (layer_norm(mid_agg) * mid_gain).astype(jnp.bfloat16)
    latent_two = (latent.astype(jnp.float32) + mm(mid_norm, mid_node)).astype(jnp.bfloat16)
    dec_proj = mm(latent_two, dec_send).astype(jnp.bfloat16)
    dec_target = mm(hidden, dec_recv).astype(jnp.bfloat16)
    dec_agg = aggregate(dec_proj, dec_target, dec_src, dec_dst, dec_live, GRID_DEV)
    dec_norm = layer_norm(dec_agg).astype(jnp.bfloat16)
    update = (hidden.astype(jnp.float32) + mm(dec_norm, dec_node)).astype(jnp.bfloat16)
    output_grad = mm(dec_norm.T, cotangent)
    pull = jax.vjp(layer_norm, dec_agg)[1]
    dec_cot = pull(mm(cotangent, dec_node.T))[0].astype(jnp.bfloat16)
    dec_src_sum, dec_dst_sum = edge_back(dec_proj, dec_target, dec_src, dec_dst, dec_live, GRID_DEV, dec_cot)
    dec_src_grad = dec_src_sum.astype(jnp.bfloat16)
    dec_dst_grad = dec_dst_sum.astype(jnp.bfloat16)
    decode_grad = mm(latent_two.T, dec_src_grad)
    latent_two_grad = mm(dec_src_grad, dec_send.T)
    pull = jax.vjp(lambda values: layer_norm(values) * mid_gain, mid_agg)[1]
    mid_cot = pull(mm(latent_two_grad.astype(jnp.bfloat16), mid_node.T))[0].astype(jnp.bfloat16)
    mid_src_sum, mid_dst_sum = edge_back(mid_proj, mid_target, mid_src, mid_dst, mid_live, MESH_DEV, mid_cot)
    mid_src_grad = mid_src_sum.astype(jnp.bfloat16)
    mid_dst_grad = mid_dst_sum.astype(jnp.bfloat16)
    process_grad = mm(latent.T, mid_src_grad)
    latent_grad = (latent_two_grad + mm(mid_src_grad, mid_send.T) + mm(mid_dst_grad, mid_recv.T)).astype(jnp.bfloat16)
    pull = jax.vjp(layer_norm, enc_agg)[1]
    enc_cot = pull(mm(latent_grad, enc_node.T))[0].astype(jnp.bfloat16)
    enc_src_sum, unused_dst = edge_back(enc_proj, enc_target, enc_src, enc_dst, enc_live, MESH_DEV, enc_cot)
    enc_src_grad = enc_src_sum.astype(jnp.bfloat16)
    encode_grad = mm(hidden.T, enc_src_grad)
    hidden_grad = cotangent.astype(jnp.float32) + mm(enc_src_grad, enc_send.T) + mm(dec_dst_grad, dec_recv.T)
    pre_grad = (hidden_grad * silu_slope(pre_act)).astype(jnp.bfloat16)
    embed_grad = mm(grid_in, pre_grad)
    return (update, embed_grad, encode_grad, process_grad, decode_grad, output_grad)
```

```python
import functools

import jax
import jax.numpy as jnp
from jax import lax
from jax.experimental import pallas as pl
from jax.experimental.pallas import tpu as pltpu
from jax.sharding import PartitionSpec as P

EPSILON = 1e-05
F32 = jnp.float32
BF16 = jnp.bfloat16


def dot(left, right, dims):
    return lax.dot_general(left, right, (dims, ((), ())), preferred_element_type=F32)


def mm(left, right):
    return dot(left, right, ((1,), (0,)))


def mm_right_t(left, right):
    return dot(left, right, ((1,), (1,)))


def mm_left_t(left, right):
    return dot(left, right, ((0,), (0,)))


def normed(values):
    center = values - jnp.mean(values, axis=-1, keepdims=True)
    scale = lax.rsqrt(jnp.mean(center * center, axis=-1, keepdims=True) + EPSILON)
    return center * scale, scale


def norm_pull(unit, scale, grad):
    inner = jnp.mean(grad * unit, axis=-1, keepdims=True)
    return scale * (grad - jnp.mean(grad, axis=-1, keepdims=True) - unit * inner)


def active(values):
    half = 0.5 * jnp.tanh(0.5 * values)
    sigma = 0.5 + half
    message = values * sigma
    return message, sigma + message * (0.5 - half)


def picks(index, rows):
    places = lax.broadcasted_iota(jnp.int32, (rows, index.shape[1]), 0)
    return jnp.where(places == index, 1.0, 0.0).astype(BF16)


INPUTS = (
    "mesh_init",
    "enc_recv",
    "enc_from",
    "enc_into",
    "enc_count",
    "grid_in",
    "embed_weight",
    "enc_send",
    "mid_from",
    "mid_into",
    "mid_count",
    "dec_from",
    "dec_into",
    "dec_count",
    "dec_recv",
    "enc_node",
    "mid_send",
    "mid_recv",
    "cotangent",
    "dec_node",
    "mid_gain",
    "mid_node",
    "dec_send",
)
OUTPUTS = (
    "update",
    "process_grad",
    "decode_grad",
    "output_grad",
    "encode_grad",
    "embed_grad",
)


class Refs:
    def __init__(self, names, refs):
        self.__dict__.update(zip(names, refs, strict=True))


def kernel(n, names, *refs):
    r = Refs(names, refs)
    me = lax.axis_index("mesh")
    left = lax.rem(me + n - 1, n)
    right = lax.rem(me + 1, n)
    core = lax.rem(me, 2)
    chip = me // 2
    chips = n // 2
    partner = me + 1 - 2 * core
    quad = lax.rem(chip, 4)
    group = chip // 4
    groups = chips // 4
    grid_rows, width = r.hidden.shape
    mesh_rows = r.mesh_init.shape[0]

    barrier = pltpu.get_barrier_semaphore()

    def greet(device):
        pl.semaphore_signal(
            barrier, inc=1, device_id={"mesh": device}, device_id_type=pl.DeviceIdType.MESH
        )

    greet(lax.rem(me + n - 1 + 2 * core, n))
    greet(partner)

    @pl.loop(1, chips)
    def _(step):
        greet(2 * lax.rem(chip + step, chips) + core)

    loads = {}
    for i, name in enumerate(INPUTS):
        loads[name] = pltpu.make_async_copy(
            getattr(r, name + "_hbm"), getattr(r, name), r.load_sem.at[i]
        )
        loads[name].start()

    def ready(*wanted):
        for name in wanted:
            loads[name].wait()

    def remote(src, dst, send, recv, device):
        return pltpu.make_async_remote_copy(
            src_ref=src,
            dst_ref=dst,
            send_sem=send,
            recv_sem=recv,
            device_id={"mesh": device},
            device_id_type=pl.DeviceIdType.MESH,
        )

    def to_left(which, src, dst):
        return remote(src, dst, r.near_send.at[which, 0], r.near_recv.at[which, 1], left)

    def to_right(which, src, dst):
        return remote(src, dst, r.near_send.at[which, 1], r.near_recv.at[which, 0], right)

    def near_arrive(which, first, second):
        to_right(which, first, first).wait_recv()
        to_left(which, second, second).wait_recv()

    sent = []

    def start(*copies):
        for copy in copies:
            copy.start()
            sent.append(copy)

    def across(which, table, owner, peer, slot):
        rows = table.at[owner]
        return remote(
            rows, rows, r.all_send.at[which, peer], r.all_recv.at[which, slot], 2 * peer + core
        )

    def beside(which, table, owner, slot):
        rows = table.at[owner]
        return remote(rows, rows, r.pass_send.at[which, slot], r.pass_recv.at[which, slot], partner)

    def gather_start(which, table):
        @pl.loop(1, chips)
        def _(step):
            across(which, table, me, lax.rem(chip + step, chips), chip).start()

        beside(which, table, me, chip).start()

    def gather_pass(which, table):
        @pl.loop(1, chips)
        def _(step):
            peer = lax.rem(chip + step, chips)
            owner = 2 * peer + core
            across(which, table, owner, peer, peer).wait_recv()
            beside(which, table, owner, peer).start()

    def gather_take(which, table):
        @pl.loop(0, chips)
        def _(slot):
            beside(which, table, 2 * slot + 1 - core, slot).wait_recv()

    def gather_sent(which, table):
        @pl.loop(1, chips)
        def _(step):
            across(which, table, me, lax.rem(chip + step, chips), chip).wait_send()

        @pl.loop(0, chips)
        def _(slot):
            beside(which, table, 2 * slot + core, slot).wait_send()

    finals = (r.output_grad, r.encode_grad, r.embed_grad)
    piece = r.terms.shape[3]

    def pair_copy(k, j):
        return remote(
            r.terms.at[k, 1 - core, j], r.halves.at[k, j], r.pair_send.at[k, j], r.pair_recv.at[k, j], partner
        )

    def quad_copy(k, j, slot):
        return remote(
            r.paired.at[k, j],
            r.quads.at[k, slot],
            r.quad_send.at[k, j],
            r.quad_recv.at[k, slot],
            2 * (group * 4 + j) + core,
        )

    def cross_copy(k, other, slot):
        mine = r.crossed.at[k, slot]
        return remote(
            mine, mine, r.cross_send.at[k, other], r.cross_recv.at[k, slot], 2 * (other * 4 + quad) + core
        )

    def fan_copy(k, j, slot):
        mine = finals[k].at[core, slot]
        return remote(
            mine, mine, r.fan_send.at[k, j], r.fan_recv.at[k, slot], 2 * (group * 4 + j) + core
        )

    def home_copy(k, side, j):
        mine = finals[k].at[side, j]
        return remote(mine, mine, r.home_send.at[k, j], r.home_recv.at[k, j], partner)

    def put_term(k, value):
        rows = value.shape[0]
        value = value.astype(BF16)
        for side in range(2):
            for j in range(4):
                low = (side * 4 + j) * piece
                high = min(low + piece, rows)
                if high - low < piece:
                    r.terms[k, side, j] = jnp.zeros((piece, width), BF16)
                if low < high:
                    r.terms[k, side, j, 0 : high - low] = value[low:high]

        @pl.loop(1, 5)
        def _(step):
            pair_copy(k, lax.rem(quad + step, 4)).start()

    def pair_add(k, j):
        pair_copy(k, j).wait_recv()
        both = r.terms[k, core, j].astype(F32) + r.halves[k, j].astype(F32)
        r.paired[k, j] = both.astype(BF16)

    def quad_start(k):
        @pl.loop(1, 4)
        def _(step):
            j = lax.rem(quad + step, 4)
            pair_add(k, j)
            quad_copy(k, j, quad).start()

        pair_add(k, quad)

    def cross_start(k):
        def add(step, total):
            j = lax.rem(quad + step, 4)
            quad_copy(k, j, j).wait_recv()
            return total + r.quads[k, j].astype(F32)

        total = lax.fori_loop(1, 4, add, r.paired[k, quad].astype(F32))
        r.crossed[k, group] = total.astype(BF16)

        @pl.loop(1, groups)
        def _(step):
            cross_copy(k, lax.rem(group + step, groups), group).start()

    def fan_start(k):
        @pl.loop(1, groups)
        def _(step):
            other = lax.rem(group + step, groups)
            cross_copy(k, other, other).wait_recv()

        def add(other, total):
            return total + r.crossed[k, other].astype(F32)

        total = lax.fori_loop(1, groups, add, r.crossed[k, 0].astype(F32))
        finals[k][core, quad] = total.astype(BF16)

        @pl.loop(1, 4)
        def _(step):
            fan_copy(k, lax.rem(quad + step, 4), quad).start()

        home_copy(k, core, quad).start()

    def home_start(k):
        @pl.loop(1, 4)
        def _(step):
            j = lax.rem(quad + step, 4)
            fan_copy(k, j, j).wait_recv()
            home_copy(k, core, j).start()

    def home_take(k):
        @pl.loop(0, 4)
        def _(j):
            home_copy(k, 1 - core, j).wait_recv()

    def term_sent(k):
        @pl.loop(0, 4)
        def _(j):
            pair_copy(k, j).wait_send()
            home_copy(k, core, j).wait_send()

        @pl.loop(1, 4)
        def _(step):
            j = lax.rem(quad + step, 4)
            quad_copy(k, j, quad).wait_send()
            fan_copy(k, j, quad).wait_send()

        @pl.loop(1, groups)
        def _(step):
            cross_copy(k, lax.rem(group + step, groups), group).wait_send()

    def masked(row, count):
        return jnp.where(lax.broadcasted_iota(jnp.int32, row.shape, 1) < count, row, -1)

    ready("mesh_init", "enc_recv", "enc_from", "enc_into", "enc_count")
    r.enc_pack[...] = jnp.zeros(r.enc_pack.shape, jnp.int32)
    r.enc_pack[0:3] = r.enc_from[...]
    for j in range(3):
        r.enc_pack[3 + j : 4 + j] = masked(r.enc_into[j : j + 1], r.enc_count[0:1, j : j + 1])
    r.targets[1] = mm(r.mesh_init[...], r.enc_recv[...]).astype(BF16)
    pl.semaphore_wait(barrier, chips + 1)
    start(
        to_left(1, r.targets.at[1], r.targets.at[2]),
        to_right(1, r.targets.at[1], r.targets.at[0]),
        to_left(0, r.enc_pack, r.packs.at[1]),
        to_right(0, r.enc_pack, r.packs.at[0]),
    )

    def enc_table(k, pack, row):
        r.enc_source[k] = picks(pack[row : row + 1], grid_rows)
        r.enc_table[k] = picks(pack[row + 3 : row + 4], mesh_rows)

    def enc_forward(k):
        inputs = mm_left_t(r.enc_source[k], r.enc_proj[...]) + mm_left_t(r.enc_table[k], r.targets[k])
        message, r.enc_slope[k] = active(inputs)
        r.agg_parts[k] = mm(r.enc_table[k], message.astype(BF16))

    enc_table(1, r.enc_pack, 1)
    ready("grid_in", "embed_weight")
    message, r.pre_slope[...] = active(mm_left_t(r.grid_in[...], r.embed_weight[...]))
    r.hidden[...] = message.astype(BF16)
    ready("enc_send")
    r.enc_proj[...] = mm(r.hidden[...], r.enc_send[...]).astype(BF16)

    near_arrive(0, r.packs.at[0], r.packs.at[1])
    near_arrive(1, r.targets.at[0], r.targets.at[2])
    enc_table(0, r.packs.at[0], 2)
    enc_forward(0)
    start(to_left(2, r.agg_parts.at[0], r.agg_near.at[1]))
    enc_table(2, r.packs.at[1], 0)
    enc_forward(2)
    start(to_right(2, r.agg_parts.at[2], r.agg_near.at[0]))

    ready("mid_from", "mid_into", "mid_count")
    cap = r.mid_from.shape[1]
    slots = n * cap
    spot = lax.broadcasted_iota(jnp.int32, (n, n), 0)
    diagonal = spot == lax.broadcasted_iota(jnp.int32, (n, n), 1)
    held = jnp.sum(jnp.where(diagonal, r.mid_count[...], 0), axis=1, keepdims=True)
    lane = lax.broadcasted_iota(jnp.int32, (n, cap), 1)
    r.codes[me] = jnp.where(lane < held, r.mid_into[...] * mesh_rows + r.mid_from[...], -1)
    gather_start(4, r.codes)
    enc_forward(1)

    ready("dec_from", "dec_into", "dec_count", "dec_recv")
    for j in range(3):
        r.dec_source[j] = picks(r.dec_from[j : j + 1], mesh_rows)
        r.dec_table[j] = picks(masked(r.dec_into[j : j + 1], r.dec_count[0:1, j : j + 1]), grid_rows)
    dec_target = mm(r.hidden[...], r.dec_recv[...]).astype(BF16)
    for j in range(3):
        r.dec_inputs[j] = mm_left_t(r.dec_table[j], dec_target)

    ready("enc_node")
    near_arrive(2, r.agg_near.at[0], r.agg_near.at[1])
    enc_unit, enc_scale = normed(r.agg_parts[1] + r.agg_near[0] + r.agg_near[1])
    latent = (r.mesh_init[...].astype(F32) + mm(enc_unit.astype(BF16), r.enc_node[...])).astype(BF16)
    r.lat_all[me] = latent
    gather_start(0, r.lat_all)

    gather_pass(4, r.codes)
    ready("cotangent", "dec_node")
    r.cot_node[...] = mm_right_t(r.cotangent[...], r.dec_node[...])
    gather_take(4, r.codes)
    spot = lax.broadcasted_iota(jnp.int32, (cap, slots), 1)
    lane = lax.broadcasted_iota(jnp.int32, (cap, slots), 0)
    spread = jnp.where(lax.rem(spot, cap) == lane, 1.0, 0.0).astype(BF16)
    spot = lax.broadcasted_iota(jnp.int32, (n, slots), 1) // cap
    own = jnp.where(spot == lax.broadcasted_iota(jnp.int32, (n, slots), 0), 1.0, 0.0)
    first = lax.broadcasted_iota(jnp.int32, (1, slots), 1) // cap * mesh_rows

    def decoded(codes):
        wide = mm(codes.astype(F32).astype(BF16), spread)
        code = jnp.sum(wide * own, axis=0, keepdims=True)
        into = jnp.floor((code + 0.5) * (1.0 / mesh_rows))
        return (code - into * mesh_rows).astype(jnp.int32), into.astype(jnp.int32)

    for b, block in enumerate((left, me, right)):
        sender, into = decoded(r.codes[block])
        r.mid_source[b] = picks(sender + first, n * mesh_rows)
        r.mid_table[b] = picks(into, mesh_rows)
    sender, into = decoded(r.codes[:, pl.ds(me, 1), :].reshape(n, cap))
    r.out_source[...] = picks(sender, mesh_rows)
    r.out_table[...] = picks(jnp.where(into < 0, -1, into + first), n * mesh_rows)

    tall = (n * mesh_rows, width)
    ready("mid_send", "mid_recv", "mid_gain", "mid_node", "dec_send")
    gather_pass(0, r.lat_all)
    gather_take(0, r.lat_all)
    r.mid_proj[...] = mm(r.lat_all[...].reshape(tall), r.mid_send[...]).astype(BF16)
    r.mid_target[...] = (
        mm(r.lat_all[...].reshape(tall), r.mid_recv[...]).astype(BF16).reshape(n, mesh_rows, width)
    )
    for b, block in enumerate((left, me, right)):
        inputs = mm_left_t(r.mid_source[b], r.mid_proj[...]) + mm_left_t(
            r.mid_table[b], r.mid_target[block]
        )
        message, slope = active(inputs)
        if b == 1:
            r.mid_slope[...] = slope
        r.mid_agg[b] = mm(r.mid_table[b], message.astype(BF16))
        r.lat_near[b] = r.lat_all[block]
    near = (3 * mesh_rows, width)
    mid_unit, mid_scale = normed(r.mid_agg[...].reshape(near))
    mid_norm = (mid_unit * r.mid_gain[...]).astype(BF16)
    latent_two = (
        r.lat_near[...].reshape(near).astype(F32) + mm(mid_norm, r.mid_node[...])
    ).astype(BF16)
    r.lat2_all[me] = latent_two[mesh_rows : 2 * mesh_rows]
    gather_start(1, r.lat2_all)
    r.dec_near[...] = (
        mm(latent_two, r.dec_send[...]).astype(BF16).reshape(3, mesh_rows, width)
    )

    def dec_forward(j, total):
        inputs = r.dec_inputs[j] + mm_left_t(r.dec_source[j], r.dec_near[j])
        message, slope = active(inputs)
        r.dec_inputs[j] = slope
        return total + mm(r.dec_table[j], message.astype(BF16))

    dec_agg = lax.fori_loop(0, 3, dec_forward, jnp.zeros((grid_rows, width), F32))
    unit, scale = normed(dec_agg)
    r.dec_norm[...] = unit.astype(BF16)
    r.dec_cot[...] = norm_pull(unit, scale, r.cot_node[...]).astype(BF16)
    r.dec_dst[...] = jnp.zeros((grid_rows, width), F32)

    def dec_backward(j, carry):
        grad = (mm_left_t(r.dec_table[j], r.dec_cot[...]) * r.dec_inputs[j]).astype(BF16)
        r.dec_parts[j] = mm(r.dec_source[j], grad)
        r.dec_dst[...] += mm(r.dec_table[j], grad)
        return carry

    lax.fori_loop(0, 3, dec_backward, 0)
    start(
        to_left(3, r.dec_parts.at[0], r.dec_back.at[1]),
        to_right(3, r.dec_parts.at[2], r.dec_back.at[0]),
    )
    put_term(0, mm_left_t(r.dec_norm[...], r.cotangent[...]))
    gather_pass(1, r.lat2_all)
    inputs = mm_left_t(r.out_source[...], r.mid_proj[pl.ds(me * mesh_rows, mesh_rows)]) + mm_left_t(
        r.out_table[...], r.mid_target[...].reshape(tall)
    )
    r.out_slope[...] = active(inputs)[1]
    quad_start(0)
    r.update[...] = (
        r.hidden[...].astype(F32) + mm(r.dec_norm[...], r.dec_node[...])
    ).astype(BF16)
    near_arrive(3, r.dec_back.at[0], r.dec_back.at[1])
    dec_src = (r.dec_parts[1] + r.dec_back[0] + r.dec_back[1]).astype(BF16)
    latent_two_grad = mm_right_t(dec_src, r.dec_send[...])
    grad = mm_right_t(latent_two_grad.astype(BF16), r.mid_node[...]) * r.mid_gain[...]
    unit = mid_unit[mesh_rows : 2 * mesh_rows]
    mid_cot = norm_pull(unit, mid_scale[mesh_rows : 2 * mesh_rows], grad).astype(BF16)
    r.cot_all[me] = mid_cot
    gather_start(5, r.cot_all)
    r.dsg_all[me] = dec_src
    gather_start(2, r.dsg_all)
    grad = (mm_left_t(r.mid_table[1], mid_cot) * r.mid_slope[...]).astype(BF16)
    mid_dst = mm(r.mid_table[1], grad).astype(BF16)
    r.held_grad[0] = latent_two_grad
    r.held_grad[1] = mm_right_t(mid_dst, r.mid_recv[...])
    r.hidden_grad[...] = r.cotangent[...].astype(F32) + mm_right_t(
        r.dec_dst[...].astype(BF16), r.dec_recv[...]
    )
    gather_take(1, r.lat2_all)
    gather_pass(5, r.cot_all)
    gather_take(5, r.cot_all)
    grad = (mm_left_t(r.out_table[...], r.cot_all[...].reshape(tall)) * r.out_slope[...]).astype(BF16)
    mid_src = mm(r.out_source[...], grad).astype(BF16)
    r.msg_all[me] = mid_src
    latent_grad = (
        r.held_grad[0] + r.held_grad[1] + mm_right_t(r.msg_all[me], r.mid_send[...])
    ).astype(BF16)
    enc_cot = norm_pull(enc_unit, enc_scale, mm_right_t(latent_grad, r.enc_node[...])).astype(BF16)
    r.cots[1] = enc_cot
    start(
        to_left(4, r.cots.at[1], r.cots.at[2]),
        to_right(4, r.cots.at[1], r.cots.at[0]),
    )
    gather_start(3, r.msg_all)
    cross_start(0)
    gather_pass(2, r.dsg_all)

    def enc_backward(k):
        grad = (mm_left_t(r.enc_table[k], r.cots[k]) * r.enc_slope[k]).astype(BF16)
        return mm(r.enc_source[k], grad)

    r.enc_src[...] = enc_backward(1)
    gather_take(2, r.dsg_all)
    r.decode_grad[...] = mm_left_t(r.lat2_all[...].reshape(tall), r.dsg_all[...].reshape(tall))
    near_arrive(4, r.cots.at[0], r.cots.at[2])
    r.enc_src[...] += enc_backward(0)
    r.enc_src[...] += enc_backward(2)
    enc_src_grad = r.enc_src[...].astype(BF16)
    put_term(1, mm_left_t(r.hidden[...], enc_src_grad))
    pre_grad = (
        (r.hidden_grad[...] + mm_right_t(enc_src_grad, r.enc_send[...])) * r.pre_slope[...]
    ).astype(BF16)
    quad_start(1)
    put_term(2, mm(r.grid_in[...], pre_grad))
    fan_start(0)
    gather_pass(3, r.msg_all)
    quad_start(2)
    cross_start(1)
    gather_take(3, r.msg_all)
    r.process_grad[...] = mm_left_t(r.lat_all[...].reshape(tall), r.msg_all[...].reshape(tall))
    cross_start(2)
    home_start(0)
    fan_start(1)
    fan_start(2)
    for copy in sent:
        copy.wait_send()
    gather_sent(0, r.lat_all)
    gather_sent(1, r.lat2_all)
    gather_sent(2, r.dsg_all)
    gather_sent(3, r.msg_all)
    gather_sent(4, r.codes)
    gather_sent(5, r.cot_all)
    home_take(0)
    home_start(1)
    home_start(2)
    home_take(1)
    home_take(2)
    for k in range(3):
        term_sent(k)


def finish(update, process, decode, output, encode, embed, *refs):
    outs, wide, sem = refs[:6], refs[6:9], refs[9]
    width = output.shape[-1]
    copies = []

    def write(i, source, target):
        copies.append(pltpu.make_async_copy(source, target, sem.at[i]))
        copies[-1].start()

    write(0, update, outs[0])
    write(1, process, outs[3])
    write(2, decode, outs[4])
    for k, (held, target) in enumerate(((output, outs[5]), (encode, outs[2]), (embed, outs[1]))):
        rows = target.shape[0]
        wide[k][...] = held[...].reshape(-1, width)[:rows].astype(F32)
        write(3 + k, wide[k], target)
    for copy in copies:
        copy.wait()


def shards(
    grid_in,
    mesh_init,
    embed_weight,
    enc_send,
    enc_recv,
    enc_node,
    mid_send,
    mid_recv,
    mid_node,
    dec_send,
    dec_recv,
    dec_node,
    mid_gain,
    cotangent,
    enc_from,
    enc_into,
    enc_count,
    mid_from,
    mid_into,
    mid_count,
    dec_from,
    dec_into,
    dec_count,
):
    given = dict(locals())
    n = lax.axis_size("mesh")
    channels, grid_rows = grid_in.shape
    mesh_rows, width = mesh_init.shape
    enc_slots = enc_from.shape[1]
    dec_slots = dec_from.shape[1]
    mid_slots = n * mid_from.shape[1]
    for name in ("mid_gain", "enc_count", "mid_count", "dec_count"):
        given[name] = given[name].reshape(1, -1)
    inputs = [given[name] for name in INPUTS]
    longest = max(width, channels)
    piece = -(-longest // 128) * 16
    chips = n // 2
    groups = chips // 4

    vmem = pltpu.VMEM
    dma = pltpu.SemaphoreType.DMA
    tall = vmem((n, mesh_rows, width), BF16)
    scratch = {name: vmem(x.shape, x.dtype) for name, x in zip(INPUTS, inputs)}
    scratch.update(
        pre_slope=vmem((grid_rows, width), F32),
        hidden=vmem((grid_rows, width), BF16),
        enc_proj=vmem((grid_rows, width), BF16),
        packs=vmem((2, 8, enc_slots), jnp.int32),
        enc_pack=vmem((8, enc_slots), jnp.int32),
        enc_source=vmem((3, grid_rows, enc_slots), BF16),
        enc_table=vmem((3, mesh_rows, enc_slots), BF16),
        dec_source=vmem((3, mesh_rows, dec_slots), BF16),
        dec_table=vmem((3, grid_rows, dec_slots), BF16),
        codes=vmem((n,) + mid_from.shape, jnp.int32),
        mid_source=vmem((3, n * mesh_rows, mid_slots), BF16),
        mid_table=vmem((3, mesh_rows, mid_slots), BF16),
        out_source=vmem((mesh_rows, mid_slots), BF16),
        out_table=vmem((n * mesh_rows, mid_slots), BF16),
        targets=vmem((3, mesh_rows, width), BF16),
        enc_slope=vmem((3, enc_slots, width), F32),
        agg_parts=vmem((3, mesh_rows, width), F32),
        agg_near=vmem((2, mesh_rows, width), F32),
        cot_node=vmem((grid_rows, width), F32),
        lat_all=tall,
        lat_near=vmem((3, mesh_rows, width), BF16),
        mid_proj=vmem((n * mesh_rows, width), BF16),
        mid_target=tall,
        mid_slope=vmem((mid_slots, width), F32),
        mid_agg=vmem((3, mesh_rows, width), F32),
        out_slope=vmem((mid_slots, width), F32),
        lat2_all=tall,
        dec_near=vmem((3, mesh_rows, width), BF16),
        dec_inputs=vmem((3, dec_slots, width), F32),
        dec_norm=vmem((grid_rows, width), BF16),
        dec_cot=vmem((grid_rows, width), BF16),
        dec_parts=vmem((3, mesh_rows, width), F32),
        dec_back=vmem((2, mesh_rows, width), F32),
        dec_dst=vmem((grid_rows, width), F32),
        dsg_all=tall,
        cot_all=tall,
        msg_all=tall,
        cots=vmem((3, mesh_rows, width), BF16),
        enc_src=vmem((grid_rows, width), F32),
        held_grad=vmem((2, mesh_rows, width), F32),
        hidden_grad=vmem((grid_rows, width), F32),
        terms=vmem((3, 2, 4, piece, width), BF16),
        halves=vmem((3, 4, piece, width), BF16),
        paired=vmem((3, 4, piece, width), BF16),
        quads=vmem((3, 4, piece, width), BF16),
        crossed=vmem((3, groups, piece, width), BF16),
        load_sem=dma((len(INPUTS),)),
        near_send=dma((5, 2)),
        near_recv=dma((5, 2)),
        all_send=dma((6, chips)),
        all_recv=dma((6, chips)),
        pass_send=dma((6, chips)),
        pass_recv=dma((6, chips)),
        pair_send=dma((3, 4)),
        pair_recv=dma((3, 4)),
        quad_send=dma((3, 4)),
        quad_recv=dma((3, 4)),
        cross_send=dma((3, groups)),
        cross_recv=dma((3, groups)),
        fan_send=dma((3, 4)),
        fan_recv=dma((3, 4)),
        home_send=dma((3, 4)),
        home_recv=dma((3, 4)),
    )
    names = [name + "_hbm" for name in INPUTS] + list(OUTPUTS) + list(scratch)
    hbm = pl.BlockSpec(memory_space=pltpu.HBM)
    inside = pl.BlockSpec(memory_space=pltpu.VMEM)
    split = vmem((2, 4, piece, width), BF16)
    square = vmem((width, width), F32)
    results = pl.pallas_call(
        functools.partial(kernel, n, names),
        out_shape=(vmem((grid_rows, width), BF16), square, square, split, split, split),
        in_specs=[hbm] * len(inputs),
        out_specs=(inside,) * 6,
        scratch_shapes=list(scratch.values()),
        compiler_params=pltpu.CompilerParams(
            collective_id=0, has_side_effects=True, vmem_limit_bytes=58 << 20
        ),
    )(*(pltpu.with_memory_space_constraint(x, pltpu.HBM) for x in inputs))
    grad = jax.ShapeDtypeStruct((width, width), F32)
    return pl.pallas_call(
        finish,
        out_shape=(
            jax.ShapeDtypeStruct((grid_rows, width), BF16),
            jax.ShapeDtypeStruct((channels, width), F32),
            grad,
            grad,
            grad,
            grad,
        ),
        in_specs=[inside] * 6,
        out_specs=(hbm,) * 6,
        scratch_shapes=[square, square, vmem((channels, width), F32), dma((6,))],
        compiler_params=pltpu.CompilerParams(vmem_limit_bytes=16 << 20),
    )(*(pltpu.with_memory_space_constraint(x, pltpu.VMEM) for x in results))


def solution(mesh):
    rows = P(("parts", "mesh"), None)
    split = (P("mesh", None), P("mesh", None), P("mesh"))
    return jax.shard_map(
        shards,
        mesh=mesh,
        in_specs=(P(None, ("parts", "mesh")), rows) + (P(),) * 11 + (rows,) + split * 3,
        out_specs=(rows,) + (P("parts", None),) * 5,
        check_vma=False,
    )
```

```python
import functools

import jax
import jax.numpy as jnp
from jax import lax
from jax.experimental import pallas as pl
from jax.experimental.pallas import tpu as pltpu
from jax.sharding import PartitionSpec as P

EPSILON = 1e-05
F32 = jnp.float32
BF16 = jnp.bfloat16


def dot(left, right, dims):
    return lax.dot_general(left, right, (dims, ((), ())), preferred_element_type=F32)


def mm(left, right):
    return dot(left, right, ((1,), (0,)))


def mm_right_t(left, right):
    return dot(left, right, ((1,), (1,)))


def mm_left_t(left, right):
    return dot(left, right, ((0,), (0,)))


def normed(values):
    center = values - jnp.mean(values, axis=-1, keepdims=True)
    scale = lax.rsqrt(jnp.mean(center * center, axis=-1, keepdims=True) + EPSILON)
    return center * scale, scale


def norm_pull(unit, scale, grad):
    inner = jnp.mean(grad * unit, axis=-1, keepdims=True)
    return scale * (grad - jnp.mean(grad, axis=-1, keepdims=True) - unit * inner)


def active(values):
    half = 0.5 * jnp.tanh(0.5 * values)
    sigma = 0.5 + half
    message = values * sigma
    return message, sigma + message * (0.5 - half)


def picks(index, rows):
    places = lax.broadcasted_iota(jnp.int32, (rows, index.shape[1]), 0)
    return jnp.where(places == index, 1.0, 0.0).astype(BF16)


INPUTS = (
    "mesh_init",
    "enc_recv",
    "enc_from",
    "enc_into",
    "enc_count",
    "grid_in",
    "embed_weight",
    "enc_send",
    "mid_from",
    "mid_into",
    "mid_count",
    "dec_from",
    "dec_into",
    "dec_count",
    "dec_recv",
    "enc_node",
    "mid_send",
    "mid_recv",
    "cotangent",
    "dec_node",
    "mid_gain",
    "mid_node",
    "dec_send",
)
OUTPUTS = (
    "update",
    "process_grad",
    "decode_grad",
    "output_grad",
    "encode_grad",
    "embed_grad",
)


class Refs:
    def __init__(self, names, refs):
        self.__dict__.update(zip(names, refs, strict=True))


def kernel(n, names, *refs):
    r = Refs(names, refs)
    me = lax.axis_index("mesh")
    left = lax.rem(me + n - 1, n)
    right = lax.rem(me + 1, n)
    core = lax.rem(me, 2)
    chip = me // 2
    chips = n // 2
    partner = me + 1 - 2 * core
    quad = lax.rem(chip, 4)
    group = chip // 4
    groups = chips // 4
    grid_rows, width = r.hidden.shape
    mesh_rows = r.mesh_init.shape[0]

    barrier = pltpu.get_barrier_semaphore()

    def greet(device):
        pl.semaphore_signal(
            barrier, inc=1, device_id={"mesh": device}, device_id_type=pl.DeviceIdType.MESH
        )

    greet(lax.rem(me + n - 1 + 2 * core, n))
    greet(partner)

    @pl.loop(1, chips)
    def _(step):
        greet(2 * lax.rem(chip + step, chips) + core)

    loads = {}
    for i, name in enumerate(INPUTS):
        loads[name] = pltpu.make_async_copy(
            getattr(r, name + "_hbm"), getattr(r, name), r.load_sem.at[i]
        )
        loads[name].start()

    def ready(*wanted):
        for name in wanted:
            loads[name].wait()

    def remote(src, dst, send, recv, device):
        return pltpu.make_async_remote_copy(
            src_ref=src,
            dst_ref=dst,
            send_sem=send,
            recv_sem=recv,
            device_id={"mesh": device},
            device_id_type=pl.DeviceIdType.MESH,
        )

    def to_left(which, src, dst):
        return remote(src, dst, r.near_send.at[which, 0], r.near_recv.at[which, 1], left)

    def to_right(which, src, dst):
        return remote(src, dst, r.near_send.at[which, 1], r.near_recv.at[which, 0], right)

    def near_arrive(which, first, second):
        to_right(which, first, first).wait_recv()
        to_left(which, second, second).wait_recv()

    sent = []

    def start(*copies):
        for copy in copies:
            copy.start()
            sent.append(copy)

    def across(which, table, owner, peer, slot):
        rows = table.at[owner]
        return remote(
            rows, rows, r.all_send.at[which, peer], r.all_recv.at[which, slot], 2 * peer + core
        )

    def beside(which, table, owner, slot):
        rows = table.at[owner]
        return remote(rows, rows, r.pass_send.at[which, slot], r.pass_recv.at[which, slot], partner)

    def gather_start(which, table):
        @pl.loop(1, chips)
        def _(step):
            across(which, table, me, lax.rem(chip + step, chips), chip).start()

        beside(which, table, me, chip).start()

    def gather_pass(which, table):
        @pl.loop(1, chips)
        def _(step):
            peer = lax.rem(chip + step, chips)
            owner = 2 * peer + core
            across(which, table, owner, peer, peer).wait_recv()
            beside(which, table, owner, peer).start()

    def gather_take(which, table):
        @pl.loop(0, chips)
        def _(slot):
            beside(which, table, 2 * slot + 1 - core, slot).wait_recv()

    def gather_sent(which, table):
        @pl.loop(1, chips)
        def _(step):
            across(which, table, me, lax.rem(chip + step, chips), chip).wait_send()

        @pl.loop(0, chips)
        def _(slot):
            beside(which, table, 2 * slot + core, slot).wait_send()

    finals = (r.output_grad, r.encode_grad, r.embed_grad)
    piece = r.terms.shape[3]

    def pair_copy(k, j):
        return remote(
            r.terms.at[k, 1 - core, j], r.halves.at[k, j], r.pair_send.at[k, j], r.pair_recv.at[k, j], partner
        )

    def quad_copy(k, j, slot):
        return remote(
            r.paired.at[k, j],
            r.quads.at[k, slot],
            r.quad_send.at[k, j],
            r.quad_recv.at[k, slot],
            2 * (group * 4 + j) + core,
        )

    def cross_copy(k, other, slot):
        mine = r.crossed.at[k, slot]
        return remote(
            mine, mine, r.cross_send.at[k, other], r.cross_recv.at[k, slot], 2 * (other * 4 + quad) + core
        )

    def fan_copy(k, j, slot):
        mine = finals[k].at[core, slot]
        return remote(
            mine, mine, r.fan_send.at[k, j], r.fan_recv.at[k, slot], 2 * (group * 4 + j) + core
        )

    def home_copy(k, side, j):
        mine = finals[k].at[side, j]
        return remote(mine, mine, r.home_send.at[k, j], r.home_recv.at[k, j], partner)

    def put_term(k, value):
        rows = value.shape[0]
        value = value.astype(BF16)
        for side in range(2):
            for j in range(4):
                low = (side * 4 + j) * piece
                high = min(low + piece, rows)
                if high - low < piece:
                    r.terms[k, side, j] = jnp.zeros((piece, width), BF16)
                if low < high:
                    r.terms[k, side, j, 0 : high - low] = value[low:high]

        @pl.loop(1, 5)
        def _(step):
            pair_copy(k, lax.rem(quad + step, 4)).start()

    def pair_add(k, j):
        pair_copy(k, j).wait_recv()
        both = r.terms[k, core, j].astype(F32) + r.halves[k, j].astype(F32)
        r.paired[k, j] = both.astype(BF16)

    def quad_start(k):
        @pl.loop(1, 4)
        def _(step):
            j = lax.rem(quad + step, 4)
            pair_add(k, j)
            quad_copy(k, j, quad).start()

        pair_add(k, quad)

    def cross_start(k):
        def add(step, total):
            j = lax.rem(quad + step, 4)
            quad_copy(k, j, j).wait_recv()
            return total + r.quads[k, j].astype(F32)

        total = lax.fori_loop(1, 4, add, r.paired[k, quad].astype(F32))
        r.crossed[k, group] = total.astype(BF16)

        @pl.loop(1, groups)
        def _(step):
            cross_copy(k, lax.rem(group + step, groups), group).start()

    def fan_start(k):
        @pl.loop(1, groups)
        def _(step):
            other = lax.rem(group + step, groups)
            cross_copy(k, other, other).wait_recv()

        def add(other, total):
            return total + r.crossed[k, other].astype(F32)

        total = lax.fori_loop(1, groups, add, r.crossed[k, 0].astype(F32))
        finals[k][core, quad] = total.astype(BF16)

        @pl.loop(1, 4)
        def _(step):
            fan_copy(k, lax.rem(quad + step, 4), quad).start()

        home_copy(k, core, quad).start()

    def home_start(k):
        @pl.loop(1, 4)
        def _(step):
            j = lax.rem(quad + step, 4)
            fan_copy(k, j, j).wait_recv()
            home_copy(k, core, j).start()

    def home_take(k):
        @pl.loop(0, 4)
        def _(j):
            home_copy(k, 1 - core, j).wait_recv()

    def term_sent(k):
        @pl.loop(0, 4)
        def _(j):
            pair_copy(k, j).wait_send()
            home_copy(k, core, j).wait_send()

        @pl.loop(1, 4)
        def _(step):
            j = lax.rem(quad + step, 4)
            quad_copy(k, j, quad).wait_send()
            fan_copy(k, j, quad).wait_send()

        @pl.loop(1, groups)
        def _(step):
            cross_copy(k, lax.rem(group + step, groups), group).wait_send()

    def masked(row, count):
        return jnp.where(lax.broadcasted_iota(jnp.int32, row.shape, 1) < count, row, -1)

    ready("mesh_init", "enc_recv", "enc_from", "enc_into", "enc_count")
    r.enc_pack[...] = jnp.zeros(r.enc_pack.shape, jnp.int32)
    r.enc_pack[0:3] = r.enc_from[...]
    for j in range(3):
        r.enc_pack[3 + j : 4 + j] = masked(r.enc_into[j : j + 1], r.enc_count[0:1, j : j + 1])
    r.targets[1] = mm(r.mesh_init[...], r.enc_recv[...]).astype(BF16)
    pl.semaphore_wait(barrier, chips + 1)
    start(
        to_left(1, r.targets.at[1], r.targets.at[2]),
        to_right(1, r.targets.at[1], r.targets.at[0]),
        to_left(0, r.enc_pack, r.packs.at[1]),
        to_right(0, r.enc_pack, r.packs.at[0]),
    )

    def enc_table(k, pack, row):
        r.enc_source[k] = picks(pack[row : row + 1], grid_rows)
        r.enc_table[k] = picks(pack[row + 3 : row + 4], mesh_rows)

    def enc_forward(k):
        inputs = mm_left_t(r.enc_source[k], r.enc_proj[...]) + mm_left_t(r.enc_table[k], r.targets[k])
        message, r.enc_slope[k] = active(inputs)
        r.agg_parts[k] = mm(r.enc_table[k], message.astype(BF16))

    enc_table(1, r.enc_pack, 1)
    ready("grid_in", "embed_weight")
    message, r.pre_slope[...] = active(mm_left_t(r.grid_in[...], r.embed_weight[...]))
    r.hidden[...] = message.astype(BF16)
    ready("enc_send")
    r.enc_proj[...] = mm(r.hidden[...], r.enc_send[...]).astype(BF16)

    near_arrive(0, r.packs.at[0], r.packs.at[1])
    near_arrive(1, r.targets.at[0], r.targets.at[2])
    enc_table(0, r.packs.at[0], 2)
    enc_forward(0)
    start(to_left(2, r.agg_parts.at[0], r.agg_near.at[1]))
    enc_table(2, r.packs.at[1], 0)
    enc_forward(2)
    start(to_right(2, r.agg_parts.at[2], r.agg_near.at[0]))

    ready("mid_from", "mid_into", "mid_count")
    cap = r.mid_from.shape[1]
    slots = n * cap
    spot = lax.broadcasted_iota(jnp.int32, (n, n), 0)
    diagonal = spot == lax.broadcasted_iota(jnp.int32, (n, n), 1)
    held = jnp.sum(jnp.where(diagonal, r.mid_count[...], 0), axis=1, keepdims=True)
    lane = lax.broadcasted_iota(jnp.int32, (n, cap), 1)
    r.codes[me] = jnp.where(lane < held, r.mid_into[...] * mesh_rows + r.mid_from[...], -1)
    gather_start(4, r.codes)
    enc_forward(1)

    ready("dec_from", "dec_into", "dec_count", "dec_recv")
    for j in range(3):
        r.dec_source[j] = picks(r.dec_from[j : j + 1], mesh_rows)
        r.dec_table[j] = picks(masked(r.dec_into[j : j + 1], r.dec_count[0:1, j : j + 1]), grid_rows)
    dec_target = mm(r.hidden[...], r.dec_recv[...]).astype(BF16)
    for j in range(3):
        r.dec_inputs[j] = mm_left_t(r.dec_table[j], dec_target)

    ready("enc_node")
    near_arrive(2, r.agg_near.at[0], r.agg_near.at[1])
    enc_unit, enc_scale = normed(r.agg_parts[1] + r.agg_near[0] + r.agg_near[1])
    latent = (r.mesh_init[...].astype(F32) + mm(enc_unit.astype(BF16), r.enc_node[...])).astype(BF16)
    r.lat_all[me] = latent
    gather_start(0, r.lat_all)

    gather_pass(4, r.codes)
    ready("cotangent", "dec_node")
    r.cot_node[...] = mm_right_t(r.cotangent[...], r.dec_node[...])
    gather_take(4, r.codes)
    spot = lax.broadcasted_iota(jnp.int32, (cap, slots), 1)
    lane = lax.broadcasted_iota(jnp.int32, (cap, slots), 0)
    spread = jnp.where(lax.rem(spot, cap) == lane, 1.0, 0.0).astype(BF16)
    spot = lax.broadcasted_iota(jnp.int32, (n, slots), 1) // cap
    own = jnp.where(spot == lax.broadcasted_iota(jnp.int32, (n, slots), 0), 1.0, 0.0)
    first = lax.broadcasted_iota(jnp.int32, (1, slots), 1) // cap * mesh_rows

    def decoded(codes):
        wide = mm(codes.astype(F32).astype(BF16), spread)
        code = jnp.sum(wide * own, axis=0, keepdims=True)
        into = jnp.floor((code + 0.5) * (1.0 / mesh_rows))
        return (code - into * mesh_rows).astype(jnp.int32), into.astype(jnp.int32)

    for b, block in enumerate((left, me, right)):
        sender, into = decoded(r.codes[block])
        r.mid_source[b] = picks(sender + first, n * mesh_rows)
        r.mid_table[b] = picks(into, mesh_rows)
    sender, into = decoded(r.codes[:, pl.ds(me, 1), :].reshape(n, cap))
    r.out_source[...] = picks(sender, mesh_rows)
    r.out_table[...] = picks(jnp.where(into < 0, -1, into + first), n * mesh_rows)

    tall = (n * mesh_rows, width)
    ready("mid_send", "mid_recv", "mid_gain", "mid_node", "dec_send")
    gather_pass(0, r.lat_all)
    gather_take(0, r.lat_all)
    r.mid_proj[...] = mm(r.lat_all[...].reshape(tall), r.mid_send[...]).astype(BF16)
    r.mid_target[...] = (
        mm(r.lat_all[...].reshape(tall), r.mid_recv[...]).astype(BF16).reshape(n, mesh_rows, width)
    )
    for b, block in enumerate((left, me, right)):
        inputs = mm_left_t(r.mid_source[b], r.mid_proj[...]) + mm_left_t(
            r.mid_table[b], r.mid_target[block]
        )
        message, slope = active(inputs)
        if b == 1:
            r.mid_slope[...] = slope
        r.mid_agg[b] = mm(r.mid_table[b], message.astype(BF16))
        r.lat_near[b] = r.lat_all[block]
    near = (3 * mesh_rows, width)
    mid_unit, mid_scale = normed(r.mid_agg[...].reshape(near))
    mid_norm = (mid_unit * r.mid_gain[...]).astype(BF16)
    latent_two = (
        r.lat_near[...].reshape(near).astype(F32) + mm(mid_norm, r.mid_node[...])
    ).astype(BF16)
    r.lat2_all[me] = latent_two[mesh_rows : 2 * mesh_rows]
    gather_start(1, r.lat2_all)
    r.dec_near[...] = (
        mm(latent_two, r.dec_send[...]).astype(BF16).reshape(3, mesh_rows, width)
    )

    def dec_forward(j, total):
        inputs = r.dec_inputs[j] + mm_left_t(r.dec_source[j], r.dec_near[j])
        message, slope = active(inputs)
        r.dec_inputs[j] = slope
        return total + mm(r.dec_table[j], message.astype(BF16))

    dec_agg = lax.fori_loop(0, 3, dec_forward, jnp.zeros((grid_rows, width), F32))
    unit, scale = normed(dec_agg)
    r.dec_norm[...] = unit.astype(BF16)
    r.dec_cot[...] = norm_pull(unit, scale, r.cot_node[...]).astype(BF16)

    def dec_backward(j):
        grad = (mm_left_t(r.dec_table[j], r.dec_cot[...]) * r.dec_inputs[j]).astype(BF16)
        r.dec_grads[j] = grad
        r.dec_parts[j] = mm(r.dec_source[j], grad)

    dec_backward(0)
    start(to_left(3, r.dec_parts.at[0], r.dec_back.at[1]))
    dec_backward(2)
    start(to_right(3, r.dec_parts.at[2], r.dec_back.at[0]))
    dec_backward(1)
    put_term(0, mm_left_t(r.dec_norm[...], r.cotangent[...]))
    gather_pass(1, r.lat2_all)
    inputs = mm_left_t(r.out_source[...], r.mid_proj[pl.ds(me * mesh_rows, mesh_rows)]) + mm_left_t(
        r.out_table[...], r.mid_target[...].reshape(tall)
    )
    r.out_slope[...] = active(inputs)[1]
    quad_start(0)
    near_arrive(3, r.dec_back.at[0], r.dec_back.at[1])
    dec_src = (r.dec_parts[1] + r.dec_back[0] + r.dec_back[1]).astype(BF16)
    latent_two_grad = mm_right_t(dec_src, r.dec_send[...])
    grad = mm_right_t(latent_two_grad.astype(BF16), r.mid_node[...]) * r.mid_gain[...]
    unit = mid_unit[mesh_rows : 2 * mesh_rows]
    mid_cot = norm_pull(unit, mid_scale[mesh_rows : 2 * mesh_rows], grad).astype(BF16)
    r.cot_all[me] = mid_cot
    gather_start(5, r.cot_all)
    r.dsg_all[me] = dec_src
    gather_start(2, r.dsg_all)
    cross_start(0)
    grad = (mm_left_t(r.mid_table[1], mid_cot) * r.mid_slope[...]).astype(BF16)
    mid_dst = mm(r.mid_table[1], grad).astype(BF16)
    r.held_grad[0] = latent_two_grad
    r.held_grad[1] = mm_right_t(mid_dst, r.mid_recv[...])
    r.dec_dst[...] = mm(r.dec_table[0], r.dec_grads[0])
    r.dec_dst[...] += mm(r.dec_table[1], r.dec_grads[1])
    r.dec_dst[...] += mm(r.dec_table[2], r.dec_grads[2])
    r.hidden_grad[...] = r.cotangent[...].astype(F32) + mm_right_t(
        r.dec_dst[...].astype(BF16), r.dec_recv[...]
    )
    gather_take(1, r.lat2_all)
    r.update[...] = (
        r.hidden[...].astype(F32) + mm(r.dec_norm[...], r.dec_node[...])
    ).astype(BF16)
    gather_pass(5, r.cot_all)
    gather_take(5, r.cot_all)
    grad = (mm_left_t(r.out_table[...], r.cot_all[...].reshape(tall)) * r.out_slope[...]).astype(BF16)
    mid_src = mm(r.out_source[...], grad).astype(BF16)
    r.msg_all[me] = mid_src
    latent_grad = (
        r.held_grad[0] + r.held_grad[1] + mm_right_t(r.msg_all[me], r.mid_send[...])
    ).astype(BF16)
    enc_cot = norm_pull(enc_unit, enc_scale, mm_right_t(latent_grad, r.enc_node[...])).astype(BF16)
    r.cots[1] = enc_cot
    start(
        to_left(4, r.cots.at[1], r.cots.at[2]),
        to_right(4, r.cots.at[1], r.cots.at[0]),
    )
    gather_start(3, r.msg_all)
    fan_start(0)
    gather_pass(2, r.dsg_all)

    def enc_backward(k):
        grad = (mm_left_t(r.enc_table[k], r.cots[k]) * r.enc_slope[k]).astype(BF16)
        return mm(r.enc_source[k], grad)

    r.enc_src[...] = enc_backward(1)
    gather_take(2, r.dsg_all)
    r.decode_grad[...] = mm_left_t(r.lat2_all[...].reshape(tall), r.dsg_all[...].reshape(tall))
    near_arrive(4, r.cots.at[0], r.cots.at[2])
    r.enc_src[...] += enc_backward(0)
    r.enc_src[...] += enc_backward(2)
    enc_src_grad = r.enc_src[...].astype(BF16)
    put_term(1, mm_left_t(r.hidden[...], enc_src_grad))
    pre_grad = (
        (r.hidden_grad[...] + mm_right_t(enc_src_grad, r.enc_send[...])) * r.pre_slope[...]
    ).astype(BF16)
    quad_start(1)
    home_start(0)
    put_term(2, mm(r.grid_in[...], pre_grad))
    gather_pass(3, r.msg_all)
    quad_start(2)
    cross_start(1)
    gather_take(3, r.msg_all)
    r.process_grad[...] = mm_left_t(r.lat_all[...].reshape(tall), r.msg_all[...].reshape(tall))
    cross_start(2)
    fan_start(1)
    fan_start(2)
    for copy in sent:
        copy.wait_send()
    gather_sent(0, r.lat_all)
    gather_sent(1, r.lat2_all)
    gather_sent(2, r.dsg_all)
    gather_sent(3, r.msg_all)
    gather_sent(4, r.codes)
    gather_sent(5, r.cot_all)
    home_take(0)
    home_start(1)
    home_start(2)
    home_take(1)
    home_take(2)
    for k in range(3):
        term_sent(k)


def finish(update, process, decode, output, encode, embed, *refs):
    outs, wide, sem = refs[:6], refs[6:9], refs[9]
    width = output.shape[-1]
    copies = []

    def write(i, source, target):
        copies.append(pltpu.make_async_copy(source, target, sem.at[i]))
        copies[-1].start()

    write(0, update, outs[0])
    write(1, process, outs[3])
    write(2, decode, outs[4])
    for k, (held, target) in enumerate(((output, outs[5]), (encode, outs[2]), (embed, outs[1]))):
        rows = target.shape[0]
        wide[k][...] = held[...].reshape(-1, width)[:rows].astype(F32)
        write(3 + k, wide[k], target)
    for copy in copies:
        copy.wait()


def shards(
    grid_in,
    mesh_init,
    embed_weight,
    enc_send,
    enc_recv,
    enc_node,
    mid_send,
    mid_recv,
    mid_node,
    dec_send,
    dec_recv,
    dec_node,
    mid_gain,
    cotangent,
    enc_from,
    enc_into,
    enc_count,
    mid_from,
    mid_into,
    mid_count,
    dec_from,
    dec_into,
    dec_count,
):
    given = dict(locals())
    n = lax.axis_size("mesh")
    channels, grid_rows = grid_in.shape
    mesh_rows, width = mesh_init.shape
    enc_slots = enc_from.shape[1]
    dec_slots = dec_from.shape[1]
    mid_slots = n * mid_from.shape[1]
    for name in ("mid_gain", "enc_count", "mid_count", "dec_count"):
        given[name] = given[name].reshape(1, -1)
    inputs = [given[name] for name in INPUTS]
    longest = max(width, channels)
    piece = -(-longest // 128) * 16
    chips = n // 2
    groups = chips // 4

    vmem = pltpu.VMEM
    dma = pltpu.SemaphoreType.DMA
    tall = vmem((n, mesh_rows, width), BF16)
    scratch = {name: vmem(x.shape, x.dtype) for name, x in zip(INPUTS, inputs)}
    scratch.update(
        pre_slope=vmem((grid_rows, width), F32),
        hidden=vmem((grid_rows, width), BF16),
        enc_proj=vmem((grid_rows, width), BF16),
        packs=vmem((2, 8, enc_slots), jnp.int32),
        enc_pack=vmem((8, enc_slots), jnp.int32),
        enc_source=vmem((3, grid_rows, enc_slots), BF16),
        enc_table=vmem((3, mesh_rows, enc_slots), BF16),
        dec_source=vmem((3, mesh_rows, dec_slots), BF16),
        dec_table=vmem((3, grid_rows, dec_slots), BF16),
        codes=vmem((n,) + mid_from.shape, jnp.int32),
        mid_source=vmem((3, n * mesh_rows, mid_slots), BF16),
        mid_table=vmem((3, mesh_rows, mid_slots), BF16),
        out_source=vmem((mesh_rows, mid_slots), BF16),
        out_table=vmem((n * mesh_rows, mid_slots), BF16),
        targets=vmem((3, mesh_rows, width), BF16),
        enc_slope=vmem((3, enc_slots, width), F32),
        agg_parts=vmem((3, mesh_rows, width), F32),
        agg_near=vmem((2, mesh_rows, width), F32),
        cot_node=vmem((grid_rows, width), F32),
        lat_all=tall,
        lat_near=vmem((3, mesh_rows, width), BF16),
        mid_proj=vmem((n * mesh_rows, width), BF16),
        mid_target=tall,
        mid_slope=vmem((mid_slots, width), F32),
        mid_agg=vmem((3, mesh_rows, width), F32),
        out_slope=vmem((mid_slots, width), F32),
        lat2_all=tall,
        dec_near=vmem((3, mesh_rows, width), BF16),
        dec_inputs=vmem((3, dec_slots, width), F32),
        dec_grads=vmem((3, dec_slots, width), BF16),
        dec_norm=vmem((grid_rows, width), BF16),
        dec_cot=vmem((grid_rows, width), BF16),
        dec_parts=vmem((3, mesh_rows, width), F32),
        dec_back=vmem((2, mesh_rows, width), F32),
        dec_dst=vmem((grid_rows, width), F32),
        dsg_all=tall,
        cot_all=tall,
        msg_all=tall,
        cots=vmem((3, mesh_rows, width), BF16),
        enc_src=vmem((grid_rows, width), F32),
        held_grad=vmem((2, mesh_rows, width), F32),
        hidden_grad=vmem((grid_rows, width), F32),
        terms=vmem((3, 2, 4, piece, width), BF16),
        halves=vmem((3, 4, piece, width), BF16),
        paired=vmem((3, 4, piece, width), BF16),
        quads=vmem((3, 4, piece, width), BF16),
        crossed=vmem((3, groups, piece, width), BF16),
        load_sem=dma((len(INPUTS),)),
        near_send=dma((5, 2)),
        near_recv=dma((5, 2)),
        all_send=dma((6, chips)),
        all_recv=dma((6, chips)),
        pass_send=dma((6, chips)),
        pass_recv=dma((6, chips)),
        pair_send=dma((3, 4)),
        pair_recv=dma((3, 4)),
        quad_send=dma((3, 4)),
        quad_recv=dma((3, 4)),
        cross_send=dma((3, groups)),
        cross_recv=dma((3, groups)),
        fan_send=dma((3, 4)),
        fan_recv=dma((3, 4)),
        home_send=dma((3, 4)),
        home_recv=dma((3, 4)),
    )
    names = [name + "_hbm" for name in INPUTS] + list(OUTPUTS) + list(scratch)
    hbm = pl.BlockSpec(memory_space=pltpu.HBM)
    inside = pl.BlockSpec(memory_space=pltpu.VMEM)
    split = vmem((2, 4, piece, width), BF16)
    square = vmem((width, width), F32)
    results = pl.pallas_call(
        functools.partial(kernel, n, names),
        out_shape=(vmem((grid_rows, width), BF16), square, square, split, split, split),
        in_specs=[hbm] * len(inputs),
        out_specs=(inside,) * 6,
        scratch_shapes=list(scratch.values()),
        compiler_params=pltpu.CompilerParams(
            collective_id=0, has_side_effects=True, vmem_limit_bytes=60 << 20
        ),
    )(*(pltpu.with_memory_space_constraint(x, pltpu.HBM) for x in inputs))
    grad = jax.ShapeDtypeStruct((width, width), F32)
    return pl.pallas_call(
        finish,
        out_shape=(
            jax.ShapeDtypeStruct((grid_rows, width), BF16),
            jax.ShapeDtypeStruct((channels, width), F32),
            grad,
            grad,
            grad,
            grad,
        ),
        in_specs=[inside] * 6,
        out_specs=(hbm,) * 6,
        scratch_shapes=[square, square, vmem((channels, width), F32), dma((6,))],
        compiler_params=pltpu.CompilerParams(vmem_limit_bytes=16 << 20),
    )(*(pltpu.with_memory_space_constraint(x, pltpu.VMEM) for x in results))


def solution(mesh):
    rows = P(("parts", "mesh"), None)
    split = (P("mesh", None), P("mesh", None), P("mesh"))
    return jax.shard_map(
        shards,
        mesh=mesh,
        in_specs=(P(None, ("parts", "mesh")), rows) + (P(),) * 11 + (rows,) + split * 3,
        out_specs=(rows,) + (P("parts", None),) * 5,
        check_vma=False,
    )
```

```python
import functools

import jax
import jax.numpy as jnp
from jax import lax
from jax.experimental import pallas as pl
from jax.experimental.pallas import tpu as pltpu
from jax.sharding import PartitionSpec as P

EPSILON = 1e-05
F32 = jnp.float32
BF16 = jnp.bfloat16


def dot(left, right, dims):
    return lax.dot_general(left, right, (dims, ((), ())), preferred_element_type=F32)


def mm(left, right):
    return dot(left, right, ((1,), (0,)))


def mm_right_t(left, right):
    return dot(left, right, ((1,), (1,)))


def mm_left_t(left, right):
    return dot(left, right, ((0,), (0,)))


def normed(values):
    center = values - jnp.mean(values, axis=-1, keepdims=True)
    scale = lax.rsqrt(jnp.mean(center * center, axis=-1, keepdims=True) + EPSILON)
    return center * scale, scale


def norm_pull(unit, scale, grad):
    inner = jnp.mean(grad * unit, axis=-1, keepdims=True)
    return scale * (grad - jnp.mean(grad, axis=-1, keepdims=True) - unit * inner)


def active(values):
    half = 0.5 * jnp.tanh(0.5 * values)
    sigma = 0.5 + half
    message = values * sigma
    return message, sigma + message * (0.5 - half)


def picks(index, rows):
    places = lax.broadcasted_iota(jnp.int32, (rows, index.shape[1]), 0)
    return jnp.where(places == index, 1.0, 0.0).astype(BF16)


INPUTS = (
    "mesh_init",
    "enc_recv",
    "enc_from",
    "enc_into",
    "enc_count",
    "grid_in",
    "embed_weight",
    "enc_send",
    "mid_from",
    "mid_into",
    "mid_count",
    "dec_from",
    "dec_into",
    "dec_count",
    "dec_recv",
    "enc_node",
    "mid_send",
    "mid_recv",
    "cotangent",
    "dec_node",
    "mid_gain",
    "mid_node",
    "dec_send",
)
OUTPUTS = (
    "update",
    "process_grad",
    "decode_grad",
    "output_grad",
    "encode_grad",
    "embed_grad",
)


class Refs:
    def __init__(self, names, refs):
        self.__dict__.update(zip(names, refs, strict=True))


def kernel(n, names, *refs):
    r = Refs(names, refs)
    me = lax.axis_index("mesh")
    left = lax.rem(me + n - 1, n)
    right = lax.rem(me + 1, n)
    core = lax.rem(me, 2)
    chip = me // 2
    chips = n // 2
    partner = me + 1 - 2 * core
    quad = lax.rem(chip, 4)
    group = chip // 4
    groups = chips // 4
    grid_rows, width = r.hidden.shape
    mesh_rows = r.mesh_init.shape[0]

    barrier = pltpu.get_barrier_semaphore()

    def greet(device):
        pl.semaphore_signal(
            barrier, inc=1, device_id={"mesh": device}, device_id_type=pl.DeviceIdType.MESH
        )

    greet(lax.rem(me + n - 1 + 2 * core, n))
    greet(partner)

    @pl.loop(1, chips)
    def _(step):
        greet(2 * lax.rem(chip + step, chips) + core)

    loads = {}
    for i, name in enumerate(INPUTS):
        loads[name] = pltpu.make_async_copy(
            getattr(r, name + "_hbm"), getattr(r, name), r.load_sem.at[i]
        )
        loads[name].start()

    def ready(*wanted):
        for name in wanted:
            loads[name].wait()

    def remote(src, dst, send, recv, device):
        return pltpu.make_async_remote_copy(
            src_ref=src,
            dst_ref=dst,
            send_sem=send,
            recv_sem=recv,
            device_id={"mesh": device},
            device_id_type=pl.DeviceIdType.MESH,
        )

    def to_left(which, src, dst):
        return remote(src, dst, r.near_send.at[which, 0], r.near_recv.at[which, 1], left)

    def to_right(which, src, dst):
        return remote(src, dst, r.near_send.at[which, 1], r.near_recv.at[which, 0], right)

    def near_arrive(which, first, second):
        to_right(which, first, first).wait_recv()
        to_left(which, second, second).wait_recv()

    sent = []

    def start(*copies):
        for copy in copies:
            copy.start()
            sent.append(copy)

    def across(which, table, owner, peer, slot):
        rows = table.at[owner]
        return remote(
            rows, rows, r.all_send.at[which, peer], r.all_recv.at[which, slot], 2 * peer + core
        )

    def beside(which, table, owner, slot):
        rows = table.at[owner]
        return remote(rows, rows, r.pass_send.at[which, slot], r.pass_recv.at[which, slot], partner)

    def gather_start(which, table):
        @pl.loop(1, chips)
        def _(step):
            across(which, table, me, lax.rem(chip + step, chips), chip).start()

        beside(which, table, me, chip).start()

    def gather_pass(which, table):
        @pl.loop(1, chips)
        def _(step):
            peer = lax.rem(chip + step, chips)
            owner = 2 * peer + core
            across(which, table, owner, peer, peer).wait_recv()
            beside(which, table, owner, peer).start()

    def gather_take(which, table):
        @pl.loop(0, chips)
        def _(slot):
            beside(which, table, 2 * slot + 1 - core, slot).wait_recv()

    def gather_sent(which, table):
        @pl.loop(1, chips)
        def _(step):
            across(which, table, me, lax.rem(chip + step, chips), chip).wait_send()

        @pl.loop(0, chips)
        def _(slot):
            beside(which, table, 2 * slot + core, slot).wait_send()

    finals = (r.output_grad, r.encode_grad, r.embed_grad)
    piece = r.terms.shape[3]

    def pair_copy(k, j):
        return remote(
            r.terms.at[k, 1 - core, j], r.halves.at[k, j], r.pair_send.at[k, j], r.pair_recv.at[k, j], partner
        )

    def quad_copy(k, j, slot):
        return remote(
            r.paired.at[k, j],
            r.quads.at[k, slot],
            r.quad_send.at[k, j],
            r.quad_recv.at[k, slot],
            2 * (group * 4 + j) + core,
        )

    def cross_copy(k, other, slot):
        mine = r.crossed.at[k, slot]
        return remote(
            mine, mine, r.cross_send.at[k, other], r.cross_recv.at[k, slot], 2 * (other * 4 + quad) + core
        )

    def fan_copy(k, j, slot):
        mine = finals[k].at[core, slot]
        return remote(
            mine, mine, r.fan_send.at[k, j], r.fan_recv.at[k, slot], 2 * (group * 4 + j) + core
        )

    def home_copy(k, side, j):
        mine = finals[k].at[side, j]
        return remote(mine, mine, r.home_send.at[k, j], r.home_recv.at[k, j], partner)

    def put_term(k, value):
        rows = value.shape[0]
        value = value.astype(BF16)
        for side in range(2):
            for j in range(4):
                low = (side * 4 + j) * piece
                high = min(low + piece, rows)
                if high - low < piece:
                    r.terms[k, side, j] = jnp.zeros((piece, width), BF16)
                if low < high:
                    r.terms[k, side, j, 0 : high - low] = value[low:high]

        @pl.loop(1, 5)
        def _(step):
            pair_copy(k, lax.rem(quad + step, 4)).start()

    def pair_add(k, j):
        pair_copy(k, j).wait_recv()
        both = r.terms[k, core, j].astype(F32) + r.halves[k, j].astype(F32)
        r.paired[k, j] = both.astype(BF16)

    def quad_start(k):
        @pl.loop(1, 4)
        def _(step):
            j = lax.rem(quad + step, 4)
            pair_add(k, j)
            quad_copy(k, j, quad).start()

        pair_add(k, quad)

    def cross_start(k):
        def add(step, total):
            j = lax.rem(quad + step, 4)
            quad_copy(k, j, j).wait_recv()
            return total + r.quads[k, j].astype(F32)

        total = lax.fori_loop(1, 4, add, r.paired[k, quad].astype(F32))
        r.crossed[k, group] = total.astype(BF16)

        @pl.loop(1, groups)
        def _(step):
            cross_copy(k, lax.rem(group + step, groups), group).start()

    def fan_start(k):
        @pl.loop(1, groups)
        def _(step):
            other = lax.rem(group + step, groups)
            cross_copy(k, other, other).wait_recv()

        def add(other, total):
            return total + r.crossed[k, other].astype(F32)

        total = lax.fori_loop(1, groups, add, r.crossed[k, 0].astype(F32))
        finals[k][core, quad] = total.astype(BF16)

        @pl.loop(1, 4)
        def _(step):
            fan_copy(k, lax.rem(quad + step, 4), quad).start()

        home_copy(k, core, quad).start()

    def home_start(k):
        @pl.loop(1, 4)
        def _(step):
            j = lax.rem(quad + step, 4)
            fan_copy(k, j, j).wait_recv()
            home_copy(k, core, j).start()

    def home_take(k):
        @pl.loop(0, 4)
        def _(j):
            home_copy(k, 1 - core, j).wait_recv()

    def term_sent(k):
        @pl.loop(0, 4)
        def _(j):
            pair_copy(k, j).wait_send()

        @pl.loop(1, 4)
        def _(step):
            quad_copy(k, lax.rem(quad + step, 4), quad).wait_send()

        @pl.loop(1, groups)
        def _(step):
            cross_copy(k, lax.rem(group + step, groups), group).wait_send()

    def final_sent(k):
        @pl.loop(1, 4)
        def _(step):
            fan_copy(k, lax.rem(quad + step, 4), quad).wait_send()

        @pl.loop(0, 4)
        def _(j):
            home_copy(k, core, j).wait_send()

    def masked(row, count):
        return jnp.where(lax.broadcasted_iota(jnp.int32, row.shape, 1) < count, row, -1)

    ready("mesh_init", "enc_recv", "enc_from", "enc_into", "enc_count")
    r.enc_pack[...] = jnp.zeros(r.enc_pack.shape, jnp.int32)
    r.enc_pack[0:3] = r.enc_from[...]
    for j in range(3):
        r.enc_pack[3 + j : 4 + j] = masked(r.enc_into[j : j + 1], r.enc_count[0:1, j : j + 1])
    r.targets[1] = mm(r.mesh_init[...], r.enc_recv[...]).astype(BF16)
    pl.semaphore_wait(barrier, chips + 1)
    start(
        to_left(1, r.targets.at[1], r.targets.at[2]),
        to_right(1, r.targets.at[1], r.targets.at[0]),
        to_left(0, r.enc_pack, r.packs.at[1]),
        to_right(0, r.enc_pack, r.packs.at[0]),
    )

    def enc_table(k, pack, row):
        r.enc_source[k] = picks(pack[row : row + 1], grid_rows)
        r.enc_table[k] = picks(pack[row + 3 : row + 4], mesh_rows)

    def enc_forward(k):
        inputs = mm_left_t(r.enc_source[k], r.enc_proj[...]) + mm_left_t(r.enc_table[k], r.targets[k])
        message, r.enc_slope[k] = active(inputs)
        return mm(r.enc_table[k], message.astype(BF16))

    enc_table(1, r.enc_pack, 1)
    ready("grid_in", "embed_weight")
    message, r.pre_slope[...] = active(mm_left_t(r.grid_in[...], r.embed_weight[...]))
    r.hidden[...] = message.astype(BF16)
    ready("enc_send")
    r.enc_proj[...] = mm(r.hidden[...], r.enc_send[...]).astype(BF16)

    near_arrive(0, r.packs.at[0], r.packs.at[1])
    near_arrive(1, r.targets.at[0], r.targets.at[2])
    enc_table(0, r.packs.at[0], 2)
    r.agg_parts[0] = enc_forward(0).astype(BF16)
    start(to_left(2, r.agg_parts.at[0], r.agg_near.at[1]))
    enc_table(2, r.packs.at[1], 0)
    r.agg_parts[2] = enc_forward(2).astype(BF16)
    start(to_right(2, r.agg_parts.at[2], r.agg_near.at[0]))

    ready("mid_from", "mid_into", "mid_count")
    cap = r.mid_from.shape[1]
    slots = n * cap
    spot = lax.broadcasted_iota(jnp.int32, (n, n), 0)
    diagonal = spot == lax.broadcasted_iota(jnp.int32, (n, n), 1)
    held = jnp.sum(jnp.where(diagonal, r.mid_count[...], 0), axis=1, keepdims=True)
    lane = lax.broadcasted_iota(jnp.int32, (n, cap), 1)
    r.codes[me] = jnp.where(lane < held, r.mid_into[...] * mesh_rows + r.mid_from[...], -1)
    gather_start(4, r.codes)
    r.agg_own[...] = enc_forward(1)

    ready("dec_from", "dec_into", "dec_count", "dec_recv")
    for j in range(3):
        r.dec_source[j] = picks(r.dec_from[j : j + 1], mesh_rows)
        r.dec_table[j] = picks(masked(r.dec_into[j : j + 1], r.dec_count[0:1, j : j + 1]), grid_rows)
    dec_target = mm(r.hidden[...], r.dec_recv[...]).astype(BF16)
    for j in range(3):
        r.dec_inputs[j] = mm_left_t(r.dec_table[j], dec_target)

    ready("enc_node")
    near_arrive(2, r.agg_near.at[0], r.agg_near.at[1])
    enc_unit, enc_scale = normed(
        r.agg_own[...] + r.agg_near[0].astype(F32) + r.agg_near[1].astype(F32)
    )
    latent = (r.mesh_init[...].astype(F32) + mm(enc_unit.astype(BF16), r.enc_node[...])).astype(BF16)
    r.lat_all[me] = latent
    gather_start(0, r.lat_all)

    gather_pass(4, r.codes)
    ready("cotangent", "dec_node")
    r.cot_node[...] = mm_right_t(r.cotangent[...], r.dec_node[...])
    gather_take(4, r.codes)
    spot = lax.broadcasted_iota(jnp.int32, (cap, slots), 1)
    lane = lax.broadcasted_iota(jnp.int32, (cap, slots), 0)
    spread = jnp.where(lax.rem(spot, cap) == lane, 1.0, 0.0).astype(BF16)
    spot = lax.broadcasted_iota(jnp.int32, (n, slots), 1) // cap
    own = jnp.where(spot == lax.broadcasted_iota(jnp.int32, (n, slots), 0), 1.0, 0.0)
    first = lax.broadcasted_iota(jnp.int32, (1, slots), 1) // cap * mesh_rows

    def decoded(codes):
        wide = mm(codes.astype(F32).astype(BF16), spread)
        code = jnp.sum(wide * own, axis=0, keepdims=True)
        into = jnp.floor((code + 0.5) * (1.0 / mesh_rows))
        return (code - into * mesh_rows).astype(jnp.int32), into.astype(jnp.int32)

    for b, block in enumerate((left, me, right)):
        sender, into = decoded(r.codes[block])
        r.mid_source[b] = picks(sender + first, n * mesh_rows)
        r.mid_table[b] = picks(into, mesh_rows)
    sender, into = decoded(r.codes[:, pl.ds(me, 1), :].reshape(n, cap))
    r.out_source[...] = picks(sender, mesh_rows)
    r.out_table[...] = picks(jnp.where(into < 0, -1, into + first), n * mesh_rows)

    tall = (n * mesh_rows, width)
    ready("mid_send", "mid_recv", "mid_gain", "mid_node", "dec_send")
    gather_pass(0, r.lat_all)
    gather_take(0, r.lat_all)
    r.mid_proj[...] = mm(r.lat_all[...].reshape(tall), r.mid_send[...]).astype(BF16)
    r.mid_target[...] = (
        mm(r.lat_all[...].reshape(tall), r.mid_recv[...]).astype(BF16).reshape(n, mesh_rows, width)
    )
    for b, block in enumerate((left, me, right)):
        inputs = mm_left_t(r.mid_source[b], r.mid_proj[...]) + mm_left_t(
            r.mid_table[b], r.mid_target[block]
        )
        message, slope = active(inputs)
        if b == 1:
            r.mid_slope[...] = slope
        r.mid_agg[b] = mm(r.mid_table[b], message.astype(BF16))
        r.lat_near[b] = r.lat_all[block]
    near = (3 * mesh_rows, width)
    mid_unit, mid_scale = normed(r.mid_agg[...].reshape(near))
    mid_norm = (mid_unit * r.mid_gain[...]).astype(BF16)
    latent_two = (
        r.lat_near[...].reshape(near).astype(F32) + mm(mid_norm, r.mid_node[...])
    ).astype(BF16)
    r.lat2_all[me] = latent_two[mesh_rows : 2 * mesh_rows]
    gather_start(1, r.lat2_all)
    r.dec_near[...] = (
        mm(latent_two, r.dec_send[...]).astype(BF16).reshape(3, mesh_rows, width)
    )

    def dec_forward(j, total):
        inputs = r.dec_inputs[j] + mm_left_t(r.dec_source[j], r.dec_near[j])
        message, slope = active(inputs)
        r.dec_inputs[j] = slope
        return total + mm(r.dec_table[j], message.astype(BF16))

    dec_agg = lax.fori_loop(0, 3, dec_forward, jnp.zeros((grid_rows, width), F32))
    unit, scale = normed(dec_agg)
    r.dec_norm[...] = unit.astype(BF16)
    r.dec_cot[...] = norm_pull(unit, scale, r.cot_node[...]).astype(BF16)

    def dec_backward(j):
        grad = (mm_left_t(r.dec_table[j], r.dec_cot[...]) * r.dec_inputs[j]).astype(BF16)
        r.dec_grads[j] = grad
        return mm(r.dec_source[j], grad)

    r.dec_parts[0] = dec_backward(0).astype(BF16)
    start(to_left(3, r.dec_parts.at[0], r.dec_back.at[1]))
    r.dec_parts[2] = dec_backward(2).astype(BF16)
    start(to_right(3, r.dec_parts.at[2], r.dec_back.at[0]))
    r.dec_own[...] = dec_backward(1)
    put_term(0, mm_left_t(r.dec_norm[...], r.cotangent[...]))
    gather_pass(1, r.lat2_all)
    inputs = mm_left_t(r.out_source[...], r.mid_proj[pl.ds(me * mesh_rows, mesh_rows)]) + mm_left_t(
        r.out_table[...], r.mid_target[...].reshape(tall)
    )
    r.out_slope[...] = active(inputs)[1]
    quad_start(0)
    near_arrive(3, r.dec_back.at[0], r.dec_back.at[1])
    dec_src = (
        r.dec_own[...] + r.dec_back[0].astype(F32) + r.dec_back[1].astype(F32)
    ).astype(BF16)
    latent_two_grad = mm_right_t(dec_src, r.dec_send[...])
    grad = mm_right_t(latent_two_grad.astype(BF16), r.mid_node[...]) * r.mid_gain[...]
    unit = mid_unit[mesh_rows : 2 * mesh_rows]
    mid_cot = norm_pull(unit, mid_scale[mesh_rows : 2 * mesh_rows], grad).astype(BF16)
    r.cot_all[me] = mid_cot
    gather_start(5, r.cot_all)
    r.dsg_all[me] = dec_src
    gather_start(2, r.dsg_all)
    cross_start(0)
    grad = (mm_left_t(r.mid_table[1], mid_cot) * r.mid_slope[...]).astype(BF16)
    mid_dst = mm(r.mid_table[1], grad).astype(BF16)
    r.held_grad[0] = latent_two_grad
    r.held_grad[1] = mm_right_t(mid_dst, r.mid_recv[...])
    r.dec_dst[...] = mm(r.dec_table[0], r.dec_grads[0])
    r.dec_dst[...] += mm(r.dec_table[1], r.dec_grads[1])
    r.dec_dst[...] += mm(r.dec_table[2], r.dec_grads[2])
    r.hidden_grad[...] = r.cotangent[...].astype(F32) + mm_right_t(
        r.dec_dst[...].astype(BF16), r.dec_recv[...]
    )
    gather_take(1, r.lat2_all)
    r.update[...] = (
        r.hidden[...].astype(F32) + mm(r.dec_norm[...], r.dec_node[...])
    ).astype(BF16)
    gather_pass(5, r.cot_all)
    gather_take(5, r.cot_all)
    grad = (mm_left_t(r.out_table[...], r.cot_all[...].reshape(tall)) * r.out_slope[...]).astype(BF16)
    mid_src = mm(r.out_source[...], grad).astype(BF16)
    r.msg_all[me] = mid_src
    latent_grad = (
        r.held_grad[0] + r.held_grad[1] + mm_right_t(r.msg_all[me], r.mid_send[...])
    ).astype(BF16)
    enc_cot = norm_pull(enc_unit, enc_scale, mm_right_t(latent_grad, r.enc_node[...])).astype(BF16)
    r.cots[1] = enc_cot
    start(
        to_left(4, r.cots.at[1], r.cots.at[2]),
        to_right(4, r.cots.at[1], r.cots.at[0]),
    )
    gather_start(3, r.msg_all)
    fan_start(0)
    gather_pass(2, r.dsg_all)

    def enc_backward(k):
        grad = (mm_left_t(r.enc_table[k], r.cots[k]) * r.enc_slope[k]).astype(BF16)
        return mm(r.enc_source[k], grad)

    r.enc_src[...] = enc_backward(1)
    gather_take(2, r.dsg_all)
    r.decode_grad[...] = mm_left_t(r.lat2_all[...].reshape(tall), r.dsg_all[...].reshape(tall))
    near_arrive(4, r.cots.at[0], r.cots.at[2])
    r.enc_src[...] += enc_backward(0)
    r.enc_src[...] += enc_backward(2)
    enc_src_grad = r.enc_src[...].astype(BF16)
    put_term(1, mm_left_t(r.hidden[...], enc_src_grad))
    quad_start(1)
    pre_grad = (
        (r.hidden_grad[...] + mm_right_t(enc_src_grad, r.enc_send[...])) * r.pre_slope[...]
    ).astype(BF16)
    home_start(0)
    gather_pass(3, r.msg_all)
    put_term(2, mm(r.grid_in[...], pre_grad))
    quad_start(2)
    cross_start(1)
    gather_take(3, r.msg_all)
    r.process_grad[...] = mm_left_t(r.lat_all[...].reshape(tall), r.msg_all[...].reshape(tall))
    cross_start(2)
    fan_start(1)
    fan_start(2)
    for copy in sent:
        copy.wait_send()
    gather_sent(0, r.lat_all)
    gather_sent(1, r.lat2_all)
    gather_sent(2, r.dsg_all)
    gather_sent(3, r.msg_all)
    gather_sent(4, r.codes)
    gather_sent(5, r.cot_all)
    for k in range(3):
        term_sent(k)
    home_take(0)
    final_sent(0)
    home_start(1)
    home_start(2)
    home_take(1)
    final_sent(1)
    home_take(2)
    final_sent(2)


def finish(update, process, decode, output, encode, embed, *refs):
    outs, wide, sem = refs[:6], refs[6:9], refs[9]
    width = output.shape[-1]
    copies = []

    def write(i, source, target):
        copies.append(pltpu.make_async_copy(source, target, sem.at[i]))
        copies[-1].start()

    write(0, update, outs[0])
    write(1, process, outs[3])
    write(2, decode, outs[4])
    for k, (held, target) in enumerate(((output, outs[5]), (encode, outs[2]), (embed, outs[1]))):
        rows = target.shape[0]
        wide[k][...] = held[...].reshape(-1, width)[:rows].astype(F32)
        write(3 + k, wide[k], target)
    for copy in copies:
        copy.wait()


def shards(
    grid_in,
    mesh_init,
    embed_weight,
    enc_send,
    enc_recv,
    enc_node,
    mid_send,
    mid_recv,
    mid_node,
    dec_send,
    dec_recv,
    dec_node,
    mid_gain,
    cotangent,
    enc_from,
    enc_into,
    enc_count,
    mid_from,
    mid_into,
    mid_count,
    dec_from,
    dec_into,
    dec_count,
):
    given = dict(locals())
    n = lax.axis_size("mesh")
    channels, grid_rows = grid_in.shape
    mesh_rows, width = mesh_init.shape
    enc_slots = enc_from.shape[1]
    dec_slots = dec_from.shape[1]
    mid_slots = n * mid_from.shape[1]
    for name in ("mid_gain", "enc_count", "mid_count", "dec_count"):
        given[name] = given[name].reshape(1, -1)
    inputs = [given[name] for name in INPUTS]
    longest = max(width, channels)
    piece = -(-longest // 128) * 16
    chips = n // 2
    groups = chips // 4

    vmem = pltpu.VMEM
    dma = pltpu.SemaphoreType.DMA
    tall = vmem((n, mesh_rows, width), BF16)
    scratch = {name: vmem(x.shape, x.dtype) for name, x in zip(INPUTS, inputs)}
    scratch.update(
        pre_slope=vmem((grid_rows, width), F32),
        hidden=vmem((grid_rows, width), BF16),
        enc_proj=vmem((grid_rows, width), BF16),
        packs=vmem((2, 8, enc_slots), jnp.int32),
        enc_pack=vmem((8, enc_slots), jnp.int32),
        enc_source=vmem((3, grid_rows, enc_slots), BF16),
        enc_table=vmem((3, mesh_rows, enc_slots), BF16),
        dec_source=vmem((3, mesh_rows, dec_slots), BF16),
        dec_table=vmem((3, grid_rows, dec_slots), BF16),
        codes=vmem((n,) + mid_from.shape, jnp.int32),
        mid_source=vmem((3, n * mesh_rows, mid_slots), BF16),
        mid_table=vmem((3, mesh_rows, mid_slots), BF16),
        out_source=vmem((mesh_rows, mid_slots), BF16),
        out_table=vmem((n * mesh_rows, mid_slots), BF16),
        targets=vmem((3, mesh_rows, width), BF16),
        enc_slope=vmem((3, enc_slots, width), F32),
        agg_parts=vmem((3, mesh_rows, width), BF16),
        agg_own=vmem((mesh_rows, width), F32),
        agg_near=vmem((2, mesh_rows, width), BF16),
        cot_node=vmem((grid_rows, width), F32),
        lat_all=tall,
        lat_near=vmem((3, mesh_rows, width), BF16),
        mid_proj=vmem((n * mesh_rows, width), BF16),
        mid_target=tall,
        mid_slope=vmem((mid_slots, width), F32),
        mid_agg=vmem((3, mesh_rows, width), F32),
        out_slope=vmem((mid_slots, width), F32),
        lat2_all=tall,
        dec_near=vmem((3, mesh_rows, width), BF16),
        dec_inputs=vmem((3, dec_slots, width), F32),
        dec_grads=vmem((3, dec_slots, width), BF16),
        dec_norm=vmem((grid_rows, width), BF16),
        dec_cot=vmem((grid_rows, width), BF16),
        dec_parts=vmem((3, mesh_rows, width), BF16),
        dec_own=vmem((mesh_rows, width), F32),
        dec_back=vmem((2, mesh_rows, width), BF16),
        dec_dst=vmem((grid_rows, width), F32),
        dsg_all=tall,
        cot_all=tall,
        msg_all=tall,
        cots=vmem((3, mesh_rows, width), BF16),
        enc_src=vmem((grid_rows, width), F32),
        held_grad=vmem((2, mesh_rows, width), F32),
        hidden_grad=vmem((grid_rows, width), F32),
        terms=vmem((3, 2, 4, piece, width), BF16),
        halves=vmem((3, 4, piece, width), BF16),
        paired=vmem((3, 4, piece, width), BF16),
        quads=vmem((3, 4, piece, width), BF16),
        crossed=vmem((3, groups, piece, width), BF16),
        load_sem=dma((len(INPUTS),)),
        near_send=dma((5, 2)),
        near_recv=dma((5, 2)),
        all_send=dma((6, chips)),
        all_recv=dma((6, chips)),
        pass_send=dma((6, chips)),
        pass_recv=dma((6, chips)),
        pair_send=dma((3, 4)),
        pair_recv=dma((3, 4)),
        quad_send=dma((3, 4)),
        quad_recv=dma((3, 4)),
        cross_send=dma((3, groups)),
        cross_recv=dma((3, groups)),
        fan_send=dma((3, 4)),
        fan_recv=dma((3, 4)),
        home_send=dma((3, 4)),
        home_recv=dma((3, 4)),
    )
    names = [name + "_hbm" for name in INPUTS] + list(OUTPUTS) + list(scratch)
    hbm = pl.BlockSpec(memory_space=pltpu.HBM)
    inside = pl.BlockSpec(memory_space=pltpu.VMEM)
    split = vmem((2, 4, piece, width), BF16)
    square = vmem((width, width), F32)
    results = pl.pallas_call(
        functools.partial(kernel, n, names),
        out_shape=(vmem((grid_rows, width), BF16), square, square, split, split, split),
        in_specs=[hbm] * len(inputs),
        out_specs=(inside,) * 6,
        scratch_shapes=list(scratch.values()),
        compiler_params=pltpu.CompilerParams(
            collective_id=0, has_side_effects=True, vmem_limit_bytes=60 << 20
        ),
    )(*(pltpu.with_memory_space_constraint(x, pltpu.HBM) for x in inputs))
    grad = jax.ShapeDtypeStruct((width, width), F32)
    return pl.pallas_call(
        finish,
        out_shape=(
            jax.ShapeDtypeStruct((grid_rows, width), BF16),
            jax.ShapeDtypeStruct((channels, width), F32),
            grad,
            grad,
            grad,
            grad,
        ),
        in_specs=[inside] * 6,
        out_specs=(hbm,) * 6,
        scratch_shapes=[square, square, vmem((channels, width), F32), dma((6,))],
        compiler_params=pltpu.CompilerParams(vmem_limit_bytes=16 << 20),
    )(*(pltpu.with_memory_space_constraint(x, pltpu.VMEM) for x in results))


def solution(mesh):
    rows = P(("parts", "mesh"), None)
    split = (P("mesh", None), P("mesh", None), P("mesh"))
    return jax.shard_map(
        shards,
        mesh=mesh,
        in_specs=(P(None, ("parts", "mesh")), rows) + (P(),) * 11 + (rows,) + split * 3,
        out_specs=(rows,) + (P("parts", None),) * 5,
        check_vma=False,
    )
```

```python
import functools

import jax
import jax.numpy as jnp
from jax import lax
from jax.experimental import pallas as pl
from jax.experimental.pallas import tpu as pltpu
from jax.sharding import PartitionSpec as P

EPSILON = 1e-05
F32 = jnp.float32
BF16 = jnp.bfloat16


def dot(left, right, dims):
    return lax.dot_general(left, right, (dims, ((), ())), preferred_element_type=F32)


def mm(left, right):
    return dot(left, right, ((1,), (0,)))


def mm_right_t(left, right):
    return dot(left, right, ((1,), (1,)))


def mm_left_t(left, right):
    return dot(left, right, ((0,), (0,)))


def normed(values):
    center = values - jnp.mean(values, axis=-1, keepdims=True)
    scale = lax.rsqrt(jnp.mean(center * center, axis=-1, keepdims=True) + EPSILON)
    return center * scale, scale


def norm_pull(unit, scale, grad):
    inner = jnp.mean(grad * unit, axis=-1, keepdims=True)
    return scale * (grad - jnp.mean(grad, axis=-1, keepdims=True) - unit * inner)


def active(values):
    half = 0.5 * jnp.tanh(0.5 * values)
    sigma = 0.5 + half
    message = values * sigma
    return message, sigma + message * (0.5 - half)


def picks(index, rows):
    places = lax.broadcasted_iota(jnp.int32, (rows, index.shape[1]), 0)
    return jnp.where(places == index, 1.0, 0.0).astype(BF16)


INPUTS = (
    "mesh_init",
    "enc_recv",
    "enc_from",
    "enc_into",
    "enc_count",
    "grid_in",
    "embed_weight",
    "enc_send",
    "mid_from",
    "mid_into",
    "mid_count",
    "dec_from",
    "dec_into",
    "dec_count",
    "dec_recv",
    "enc_node",
    "mid_send",
    "mid_recv",
    "cotangent",
    "dec_node",
    "mid_gain",
    "mid_node",
    "dec_send",
)
OUTPUTS = (
    "update",
    "process_grad",
    "decode_grad",
    "output_grad",
    "encode_grad",
    "embed_grad",
)


class Refs:
    def __init__(self, names, refs):
        self.__dict__.update(zip(names, refs, strict=True))


def kernel(n, names, *refs):
    r = Refs(names, refs)
    me = lax.axis_index("mesh")
    left = lax.rem(me + n - 1, n)
    right = lax.rem(me + 1, n)
    core = lax.rem(me, 2)
    chip = me // 2
    chips = n // 2
    partner = me + 1 - 2 * core
    quad = lax.rem(chip, 4)
    group = chip // 4
    groups = chips // 4
    grid_rows, width = r.hidden.shape
    mesh_rows = r.mesh_init.shape[0]

    barrier = pltpu.get_barrier_semaphore()

    def greet(device):
        pl.semaphore_signal(
            barrier, inc=1, device_id={"mesh": device}, device_id_type=pl.DeviceIdType.MESH
        )

    greet(lax.rem(me + n - 1 + 2 * core, n))
    greet(partner)

    @pl.loop(1, chips)
    def _(step):
        greet(2 * lax.rem(chip + step, chips) + core)

    loads = {}
    for i, name in enumerate(INPUTS):
        loads[name] = pltpu.make_async_copy(
            getattr(r, name + "_hbm"), getattr(r, name), r.load_sem.at[i]
        )
        loads[name].start()

    def ready(*wanted):
        for name in wanted:
            loads[name].wait()

    def remote(src, dst, send, recv, device):
        return pltpu.make_async_remote_copy(
            src_ref=src,
            dst_ref=dst,
            send_sem=send,
            recv_sem=recv,
            device_id={"mesh": device},
            device_id_type=pl.DeviceIdType.MESH,
        )

    def to_left(which, src, dst):
        return remote(src, dst, r.near_send.at[which, 0], r.near_recv.at[which, 1], left)

    def to_right(which, src, dst):
        return remote(src, dst, r.near_send.at[which, 1], r.near_recv.at[which, 0], right)

    def near_arrive(which, first, second):
        to_right(which, first, first).wait_recv()
        to_left(which, second, second).wait_recv()

    sent = []

    def start(*copies):
        for copy in copies:
            copy.start()
            sent.append(copy)

    def across(which, table, owner, peer, slot):
        rows = table.at[owner]
        return remote(
            rows, rows, r.all_send.at[which, peer], r.all_recv.at[which, slot], 2 * peer + core
        )

    def beside(which, table, owner, slot):
        rows = table.at[owner]
        return remote(rows, rows, r.pass_send.at[which, slot], r.pass_recv.at[which, slot], partner)

    def gather_start(which, table):
        @pl.loop(1, chips)
        def _(step):
            across(which, table, me, lax.rem(chip + step, chips), chip).start()

        beside(which, table, me, chip).start()

    def gather_pass(which, table):
        @pl.loop(1, chips)
        def _(step):
            peer = lax.rem(chip + step, chips)
            owner = 2 * peer + core
            across(which, table, owner, peer, peer).wait_recv()
            beside(which, table, owner, peer).start()

    def gather_take(which, table):
        @pl.loop(0, chips)
        def _(slot):
            beside(which, table, 2 * slot + 1 - core, slot).wait_recv()

    def gather_sent(which, table):
        @pl.loop(1, chips)
        def _(step):
            across(which, table, me, lax.rem(chip + step, chips), chip).wait_send()

        @pl.loop(0, chips)
        def _(slot):
            beside(which, table, 2 * slot + core, slot).wait_send()

    finals = (r.output_grad, r.encode_grad, r.embed_grad)
    piece = r.terms.shape[3]

    def pair_copy(k, j):
        return remote(
            r.terms.at[k, 1 - core, j], r.halves.at[k, j], r.pair_send.at[k, j], r.pair_recv.at[k, j], partner
        )

    def quad_copy(k, j, slot):
        return remote(
            r.paired.at[k, j],
            r.quads.at[k, slot],
            r.quad_send.at[k, j],
            r.quad_recv.at[k, slot],
            2 * (group * 4 + j) + core,
        )

    def cross_copy(k, other, slot):
        mine = r.crossed.at[k, slot]
        return remote(
            mine, mine, r.cross_send.at[k, other], r.cross_recv.at[k, slot], 2 * (other * 4 + quad) + core
        )

    def fan_copy(k, j, slot):
        mine = finals[k].at[core, slot]
        return remote(
            mine, mine, r.fan_send.at[k, j], r.fan_recv.at[k, slot], 2 * (group * 4 + j) + core
        )

    def home_copy(k, side, j):
        mine = finals[k].at[side, j]
        return remote(mine, mine, r.home_send.at[k, j], r.home_recv.at[k, j], partner)

    def put_term(k, value):
        rows = value.shape[0]
        value = value.astype(BF16)
        for side in range(2):
            for j in range(4):
                low = (side * 4 + j) * piece
                high = min(low + piece, rows)
                if high - low < piece:
                    r.terms[k, side, j] = jnp.zeros((piece, width), BF16)
                if low < high:
                    r.terms[k, side, j, 0 : high - low] = value[low:high]

        @pl.loop(1, 5)
        def _(step):
            pair_copy(k, lax.rem(quad + step, 4)).start()

    def pair_add(k, j):
        pair_copy(k, j).wait_recv()
        both = r.terms[k, core, j].astype(F32) + r.halves[k, j].astype(F32)
        r.paired[k, j] = both.astype(BF16)

    def quad_start(k):
        @pl.loop(1, 4)
        def _(step):
            j = lax.rem(quad + step, 4)
            pair_add(k, j)
            quad_copy(k, j, quad).start()

        pair_add(k, quad)

    def cross_start(k):
        def add(step, total):
            j = lax.rem(quad + step, 4)
            quad_copy(k, j, j).wait_recv()
            return total + r.quads[k, j].astype(F32)

        total = lax.fori_loop(1, 4, add, r.paired[k, quad].astype(F32))
        r.crossed[k, group] = total.astype(BF16)

        @pl.loop(1, groups)
        def _(step):
            cross_copy(k, lax.rem(group + step, groups), group).start()

    def fan_start(k):
        @pl.loop(1, groups)
        def _(step):
            other = lax.rem(group + step, groups)
            cross_copy(k, other, other).wait_recv()

        def add(other, total):
            return total + r.crossed[k, other].astype(F32)

        total = lax.fori_loop(1, groups, add, r.crossed[k, 0].astype(F32))
        finals[k][core, quad] = total.astype(BF16)

        @pl.loop(1, 4)
        def _(step):
            fan_copy(k, lax.rem(quad + step, 4), quad).start()

        home_copy(k, core, quad).start()

    def home_start(k):
        @pl.loop(1, 4)
        def _(step):
            j = lax.rem(quad + step, 4)
            fan_copy(k, j, j).wait_recv()
            home_copy(k, core, j).start()

    def home_take(k):
        @pl.loop(0, 4)
        def _(j):
            home_copy(k, 1 - core, j).wait_recv()

    def term_sent(k):
        @pl.loop(0, 4)
        def _(j):
            pair_copy(k, j).wait_send()

        @pl.loop(1, 4)
        def _(step):
            quad_copy(k, lax.rem(quad + step, 4), quad).wait_send()

        @pl.loop(1, groups)
        def _(step):
            cross_copy(k, lax.rem(group + step, groups), group).wait_send()

    def final_sent(k):
        @pl.loop(1, 4)
        def _(step):
            fan_copy(k, lax.rem(quad + step, 4), quad).wait_send()

        @pl.loop(0, 4)
        def _(j):
            home_copy(k, core, j).wait_send()

    def masked(row, count):
        return jnp.where(lax.broadcasted_iota(jnp.int32, row.shape, 1) < count, row, -1)

    ready("mesh_init", "enc_recv", "enc_from", "enc_into", "enc_count")
    r.enc_pack[...] = jnp.zeros(r.enc_pack.shape, jnp.int32)
    r.enc_pack[0:3] = r.enc_from[...]
    for j in range(3):
        r.enc_pack[3 + j : 4 + j] = masked(r.enc_into[j : j + 1], r.enc_count[0:1, j : j + 1])
    r.targets[1] = mm(r.mesh_init[...], r.enc_recv[...]).astype(BF16)
    pl.semaphore_wait(barrier, chips + 1)
    start(
        to_left(1, r.targets.at[1], r.targets.at[2]),
        to_right(1, r.targets.at[1], r.targets.at[0]),
        to_left(0, r.enc_pack, r.packs.at[1]),
        to_right(0, r.enc_pack, r.packs.at[0]),
    )

    def enc_table(k, pack, row):
        r.enc_source[k] = picks(pack[row : row + 1], grid_rows)
        r.enc_table[k] = picks(pack[row + 3 : row + 4], mesh_rows)

    def enc_forward(k):
        inputs = mm_left_t(r.enc_source[k], r.enc_proj[...]) + mm_left_t(r.enc_table[k], r.targets[k])
        message, r.enc_slope[k] = active(inputs)
        return mm(r.enc_table[k], message.astype(BF16))

    enc_table(1, r.enc_pack, 1)
    ready("grid_in", "embed_weight")
    message, r.pre_slope[...] = active(mm_left_t(r.grid_in[...], r.embed_weight[...]))
    r.hidden[...] = message.astype(BF16)
    ready("enc_send")
    r.enc_proj[...] = mm(r.hidden[...], r.enc_send[...]).astype(BF16)

    near_arrive(0, r.packs.at[0], r.packs.at[1])
    near_arrive(1, r.targets.at[0], r.targets.at[2])
    enc_table(0, r.packs.at[0], 2)
    r.agg_parts[0] = enc_forward(0).astype(BF16)
    start(to_left(2, r.agg_parts.at[0], r.agg_near.at[1]))
    enc_table(2, r.packs.at[1], 0)
    r.agg_parts[2] = enc_forward(2).astype(BF16)
    start(to_right(2, r.agg_parts.at[2], r.agg_near.at[0]))

    ready("mid_from", "mid_into", "mid_count")
    cap = r.mid_from.shape[1]
    slots = n * cap
    spot = lax.broadcasted_iota(jnp.int32, (n, n), 0)
    diagonal = spot == lax.broadcasted_iota(jnp.int32, (n, n), 1)
    held = jnp.sum(jnp.where(diagonal, r.mid_count[...], 0), axis=1, keepdims=True)
    lane = lax.broadcasted_iota(jnp.int32, (n, cap), 1)
    r.codes[me] = jnp.where(lane < held, r.mid_into[...] * mesh_rows + r.mid_from[...], -1)
    gather_start(4, r.codes)
    r.agg_own[...] = enc_forward(1)

    ready("dec_from", "dec_into", "dec_count", "dec_recv")
    for j in range(3):
        r.dec_source[j] = picks(r.dec_from[j : j + 1], mesh_rows)
        r.dec_table[j] = picks(masked(r.dec_into[j : j + 1], r.dec_count[0:1, j : j + 1]), grid_rows)
    dec_target = mm(r.hidden[...], r.dec_recv[...]).astype(BF16)
    for j in range(3):
        r.dec_inputs[j] = mm_left_t(r.dec_table[j], dec_target)

    ready("enc_node")
    near_arrive(2, r.agg_near.at[0], r.agg_near.at[1])
    enc_unit, enc_scale = normed(
        r.agg_own[...] + r.agg_near[0].astype(F32) + r.agg_near[1].astype(F32)
    )
    latent = (r.mesh_init[...].astype(F32) + mm(enc_unit.astype(BF16), r.enc_node[...])).astype(BF16)
    r.lat_all[me] = latent
    gather_start(0, r.lat_all)

    gather_pass(4, r.codes)
    ready("cotangent", "dec_node")
    r.cot_node[...] = mm_right_t(r.cotangent[...], r.dec_node[...])
    gather_take(4, r.codes)
    spot = lax.broadcasted_iota(jnp.int32, (cap, slots), 1)
    lane = lax.broadcasted_iota(jnp.int32, (cap, slots), 0)
    spread = jnp.where(lax.rem(spot, cap) == lane, 1.0, 0.0).astype(BF16)
    spot = lax.broadcasted_iota(jnp.int32, (n, slots), 1) // cap
    own = jnp.where(spot == lax.broadcasted_iota(jnp.int32, (n, slots), 0), 1.0, 0.0)
    first = lax.broadcasted_iota(jnp.int32, (1, slots), 1) // cap * mesh_rows

    def decoded(codes):
        wide = mm(codes.astype(F32).astype(BF16), spread)
        code = jnp.sum(wide * own, axis=0, keepdims=True)
        into = jnp.floor((code + 0.5) * (1.0 / mesh_rows))
        return (code - into * mesh_rows).astype(jnp.int32), into.astype(jnp.int32)

    for b, block in enumerate((left, me, right)):
        sender, into = decoded(r.codes[block])
        r.mid_source[b] = picks(sender + first, n * mesh_rows)
        r.mid_table[b] = picks(into, mesh_rows)
    sender, into = decoded(r.codes[:, pl.ds(me, 1), :].reshape(n, cap))
    r.out_source[...] = picks(sender, mesh_rows)
    r.out_table[...] = picks(jnp.where(into < 0, -1, into + first), n * mesh_rows)

    tall = (n * mesh_rows, width)
    ready("mid_send", "mid_recv", "mid_gain", "mid_node", "dec_send")
    gather_pass(0, r.lat_all)
    gather_take(0, r.lat_all)
    r.mid_proj[...] = mm(r.lat_all[...].reshape(tall), r.mid_send[...]).astype(BF16)
    r.mid_target[...] = (
        mm(r.lat_all[...].reshape(tall), r.mid_recv[...]).astype(BF16).reshape(n, mesh_rows, width)
    )
    for b, block in enumerate((left, me, right)):
        inputs = mm_left_t(r.mid_source[b], r.mid_proj[...]) + mm_left_t(
            r.mid_table[b], r.mid_target[block]
        )
        message, slope = active(inputs)
        if b == 1:
            r.mid_slope[...] = slope
        r.mid_agg[b] = mm(r.mid_table[b], message.astype(BF16))
        r.lat_near[b] = r.lat_all[block]
    near = (3 * mesh_rows, width)
    mid_unit, mid_scale = normed(r.mid_agg[...].reshape(near))
    mid_norm = (mid_unit * r.mid_gain[...]).astype(BF16)
    latent_two = (
        r.lat_near[...].reshape(near).astype(F32) + mm(mid_norm, r.mid_node[...])
    ).astype(BF16)
    r.lat2_all[me] = latent_two[mesh_rows : 2 * mesh_rows]
    gather_start(1, r.lat2_all)
    r.dec_near[...] = (
        mm(latent_two, r.dec_send[...]).astype(BF16).reshape(3, mesh_rows, width)
    )

    def dec_forward(j, total):
        inputs = r.dec_inputs[j] + mm_left_t(r.dec_source[j], r.dec_near[j])
        message, slope = active(inputs)
        r.dec_inputs[j] = slope
        return total + mm(r.dec_table[j], message.astype(BF16))

    dec_agg = lax.fori_loop(0, 3, dec_forward, jnp.zeros((grid_rows, width), F32))
    unit, scale = normed(dec_agg)
    r.dec_norm[...] = unit.astype(BF16)
    r.dec_cot[...] = norm_pull(unit, scale, r.cot_node[...]).astype(BF16)

    def dec_backward(j):
        grad = (mm_left_t(r.dec_table[j], r.dec_cot[...]) * r.dec_inputs[j]).astype(BF16)
        r.dec_grads[j] = grad
        return mm(r.dec_source[j], grad)

    r.dec_parts[0] = dec_backward(0).astype(BF16)
    start(to_left(3, r.dec_parts.at[0], r.dec_back.at[1]))
    r.dec_parts[2] = dec_backward(2).astype(BF16)
    start(to_right(3, r.dec_parts.at[2], r.dec_back.at[0]))
    r.dec_own[...] = dec_backward(1)
    put_term(0, mm_left_t(r.dec_norm[...], r.cotangent[...]))
    gather_pass(1, r.lat2_all)
    inputs = mm_left_t(r.out_source[...], r.mid_proj[pl.ds(me * mesh_rows, mesh_rows)]) + mm_left_t(
        r.out_table[...], r.mid_target[...].reshape(tall)
    )
    r.out_slope[...] = active(inputs)[1]
    quad_start(0)
    near_arrive(3, r.dec_back.at[0], r.dec_back.at[1])
    dec_src = (
        r.dec_own[...] + r.dec_back[0].astype(F32) + r.dec_back[1].astype(F32)
    ).astype(BF16)
    latent_two_grad = mm_right_t(dec_src, r.dec_send[...])
    grad = mm_right_t(latent_two_grad.astype(BF16), r.mid_node[...]) * r.mid_gain[...]
    unit = mid_unit[mesh_rows : 2 * mesh_rows]
    mid_cot = norm_pull(unit, mid_scale[mesh_rows : 2 * mesh_rows], grad).astype(BF16)
    r.cot_all[me] = mid_cot
    gather_start(5, r.cot_all)
    r.dsg_all[me] = dec_src
    gather_start(2, r.dsg_all)
    cross_start(0)
    grad = (mm_left_t(r.mid_table[1], mid_cot) * r.mid_slope[...]).astype(BF16)
    mid_dst = mm(r.mid_table[1], grad).astype(BF16)
    r.held_grad[0] = latent_two_grad
    r.held_grad[1] = mm_right_t(mid_dst, r.mid_recv[...])
    r.dec_dst[...] = mm(r.dec_table[0], r.dec_grads[0])
    r.dec_dst[...] += mm(r.dec_table[1], r.dec_grads[1])
    r.dec_dst[...] += mm(r.dec_table[2], r.dec_grads[2])
    r.hidden_grad[...] = r.cotangent[...].astype(F32) + mm_right_t(
        r.dec_dst[...].astype(BF16), r.dec_recv[...]
    )
    gather_take(1, r.lat2_all)
    r.update[...] = (
        r.hidden[...].astype(F32) + mm(r.dec_norm[...], r.dec_node[...])
    ).astype(BF16)
    gather_pass(5, r.cot_all)
    gather_take(5, r.cot_all)
    grad = (mm_left_t(r.out_table[...], r.cot_all[...].reshape(tall)) * r.out_slope[...]).astype(BF16)
    mid_src = mm(r.out_source[...], grad).astype(BF16)
    r.msg_all[me] = mid_src
    latent_grad = (
        r.held_grad[0] + r.held_grad[1] + mm_right_t(r.msg_all[me], r.mid_send[...])
    ).astype(BF16)
    enc_cot = norm_pull(enc_unit, enc_scale, mm_right_t(latent_grad, r.enc_node[...])).astype(BF16)
    r.cots[1] = enc_cot
    start(
        to_left(4, r.cots.at[1], r.cots.at[2]),
        to_right(4, r.cots.at[1], r.cots.at[0]),
    )
    gather_start(3, r.msg_all)
    gather_pass(2, r.dsg_all)
    fan_start(0)

    def enc_backward(k):
        grad = (mm_left_t(r.enc_table[k], r.cots[k]) * r.enc_slope[k]).astype(BF16)
        return mm(r.enc_source[k], grad)

    r.enc_src[...] = enc_backward(1)
    gather_take(2, r.dsg_all)
    r.decode_grad[...] = mm_left_t(r.lat2_all[...].reshape(tall), r.dsg_all[...].reshape(tall))
    near_arrive(4, r.cots.at[0], r.cots.at[2])
    r.enc_src[...] += enc_backward(0)
    r.enc_src[...] += enc_backward(2)
    enc_src_grad = r.enc_src[...].astype(BF16)
    put_term(1, mm_left_t(r.hidden[...], enc_src_grad))
    quad_start(1)
    pre_grad = (
        (r.hidden_grad[...] + mm_right_t(enc_src_grad, r.enc_send[...])) * r.pre_slope[...]
    ).astype(BF16)
    home_start(0)
    gather_pass(3, r.msg_all)
    put_term(2, mm(r.grid_in[...], pre_grad))
    quad_start(2)
    cross_start(1)
    gather_take(3, r.msg_all)
    r.process_grad[...] = mm_left_t(r.lat_all[...].reshape(tall), r.msg_all[...].reshape(tall))
    cross_start(2)
    fan_start(1)
    fan_start(2)
    for copy in sent:
        copy.wait_send()
    gather_sent(0, r.lat_all)
    gather_sent(1, r.lat2_all)
    gather_sent(2, r.dsg_all)
    gather_sent(3, r.msg_all)
    gather_sent(4, r.codes)
    gather_sent(5, r.cot_all)
    for k in range(3):
        term_sent(k)
    home_take(0)
    final_sent(0)
    home_start(1)
    home_start(2)
    home_take(1)
    final_sent(1)
    home_take(2)
    final_sent(2)


def finish(update, process, decode, output, encode, embed, *refs):
    outs, wide, sem = refs[:6], refs[6:9], refs[9]
    width = output.shape[-1]
    copies = []

    def write(i, source, target):
        copies.append(pltpu.make_async_copy(source, target, sem.at[i]))
        copies[-1].start()

    write(0, update, outs[0])
    write(1, process, outs[3])
    write(2, decode, outs[4])
    for k, (held, target) in enumerate(((output, outs[5]), (encode, outs[2]), (embed, outs[1]))):
        rows = target.shape[0]
        wide[k][...] = held[...].reshape(-1, width)[:rows].astype(F32)
        write(3 + k, wide[k], target)
    for copy in copies:
        copy.wait()


def shards(
    grid_in,
    mesh_init,
    embed_weight,
    enc_send,
    enc_recv,
    enc_node,
    mid_send,
    mid_recv,
    mid_node,
    dec_send,
    dec_recv,
    dec_node,
    mid_gain,
    cotangent,
    enc_from,
    enc_into,
    enc_count,
    mid_from,
    mid_into,
    mid_count,
    dec_from,
    dec_into,
    dec_count,
):
    given = dict(locals())
    n = lax.axis_size("mesh")
    channels, grid_rows = grid_in.shape
    mesh_rows, width = mesh_init.shape
    enc_slots = enc_from.shape[1]
    dec_slots = dec_from.shape[1]
    mid_slots = n * mid_from.shape[1]
    for name in ("mid_gain", "enc_count", "mid_count", "dec_count"):
        given[name] = given[name].reshape(1, -1)
    inputs = [given[name] for name in INPUTS]
    longest = max(width, channels)
    piece = -(-longest // 128) * 16
    chips = n // 2
    groups = chips // 4

    vmem = pltpu.VMEM
    dma = pltpu.SemaphoreType.DMA
    tall = vmem((n, mesh_rows, width), BF16)
    scratch = {name: vmem(x.shape, x.dtype) for name, x in zip(INPUTS, inputs)}
    scratch.update(
        pre_slope=vmem((grid_rows, width), F32),
        hidden=vmem((grid_rows, width), BF16),
        enc_proj=vmem((grid_rows, width), BF16),
        packs=vmem((2, 8, enc_slots), jnp.int32),
        enc_pack=vmem((8, enc_slots), jnp.int32),
        enc_source=vmem((3, grid_rows, enc_slots), BF16),
        enc_table=vmem((3, mesh_rows, enc_slots), BF16),
        dec_source=vmem((3, mesh_rows, dec_slots), BF16),
        dec_table=vmem((3, grid_rows, dec_slots), BF16),
        codes=vmem((n,) + mid_from.shape, jnp.int32),
        mid_source=vmem((3, n * mesh_rows, mid_slots), BF16),
        mid_table=vmem((3, mesh_rows, mid_slots), BF16),
        out_source=vmem((mesh_rows, mid_slots), BF16),
        out_table=vmem((n * mesh_rows, mid_slots), BF16),
        targets=vmem((3, mesh_rows, width), BF16),
        enc_slope=vmem((3, enc_slots, width), F32),
        agg_parts=vmem((3, mesh_rows, width), BF16),
        agg_own=vmem((mesh_rows, width), F32),
        agg_near=vmem((2, mesh_rows, width), BF16),
        cot_node=vmem((grid_rows, width), F32),
        lat_all=tall,
        lat_near=vmem((3, mesh_rows, width), BF16),
        mid_proj=vmem((n * mesh_rows, width), BF16),
        mid_target=tall,
        mid_slope=vmem((mid_slots, width), F32),
        mid_agg=vmem((3, mesh_rows, width), F32),
        out_slope=vmem((mid_slots, width), F32),
        lat2_all=tall,
        dec_near=vmem((3, mesh_rows, width), BF16),
        dec_inputs=vmem((3, dec_slots, width), F32),
        dec_grads=vmem((3, dec_slots, width), BF16),
        dec_norm=vmem((grid_rows, width), BF16),
        dec_cot=vmem((grid_rows, width), BF16),
        dec_parts=vmem((3, mesh_rows, width), BF16),
        dec_own=vmem((mesh_rows, width), F32),
        dec_back=vmem((2, mesh_rows, width), BF16),
        dec_dst=vmem((grid_rows, width), F32),
        dsg_all=tall,
        cot_all=tall,
        msg_all=tall,
        cots=vmem((3, mesh_rows, width), BF16),
        enc_src=vmem((grid_rows, width), F32),
        held_grad=vmem((2, mesh_rows, width), F32),
        hidden_grad=vmem((grid_rows, width), F32),
        terms=vmem((3, 2, 4, piece, width), BF16),
        halves=vmem((3, 4, piece, width), BF16),
        paired=vmem((3, 4, piece, width), BF16),
        quads=vmem((3, 4, piece, width), BF16),
        crossed=vmem((3, groups, piece, width), BF16),
        load_sem=dma((len(INPUTS),)),
        near_send=dma((5, 2)),
        near_recv=dma((5, 2)),
        all_send=dma((6, chips)),
        all_recv=dma((6, chips)),
        pass_send=dma((6, chips)),
        pass_recv=dma((6, chips)),
        pair_send=dma((3, 4)),
        pair_recv=dma((3, 4)),
        quad_send=dma((3, 4)),
        quad_recv=dma((3, 4)),
        cross_send=dma((3, groups)),
        cross_recv=dma((3, groups)),
        fan_send=dma((3, 4)),
        fan_recv=dma((3, 4)),
        home_send=dma((3, 4)),
        home_recv=dma((3, 4)),
    )
    names = [name + "_hbm" for name in INPUTS] + list(OUTPUTS) + list(scratch)
    hbm = pl.BlockSpec(memory_space=pltpu.HBM)
    inside = pl.BlockSpec(memory_space=pltpu.VMEM)
    split = vmem((2, 4, piece, width), BF16)
    square = vmem((width, width), F32)
    results = pl.pallas_call(
        functools.partial(kernel, n, names),
        out_shape=(vmem((grid_rows, width), BF16), square, square, split, split, split),
        in_specs=[hbm] * len(inputs),
        out_specs=(inside,) * 6,
        scratch_shapes=list(scratch.values()),
        compiler_params=pltpu.CompilerParams(
            collective_id=0, has_side_effects=True, vmem_limit_bytes=60 << 20
        ),
    )(*(pltpu.with_memory_space_constraint(x, pltpu.HBM) for x in inputs))
    grad = jax.ShapeDtypeStruct((width, width), F32)
    return pl.pallas_call(
        finish,
        out_shape=(
            jax.ShapeDtypeStruct((grid_rows, width), BF16),
            jax.ShapeDtypeStruct((channels, width), F32),
            grad,
            grad,
            grad,
            grad,
        ),
        in_specs=[inside] * 6,
        out_specs=(hbm,) * 6,
        scratch_shapes=[square, square, vmem((channels, width), F32), dma((6,))],
        compiler_params=pltpu.CompilerParams(vmem_limit_bytes=16 << 20),
    )(*(pltpu.with_memory_space_constraint(x, pltpu.VMEM) for x in results))


def solution(mesh):
    rows = P(("parts", "mesh"), None)
    split = (P("mesh", None), P("mesh", None), P("mesh"))
    return jax.shard_map(
        shards,
        mesh=mesh,
        in_specs=(P(None, ("parts", "mesh")), rows) + (P(),) * 11 + (rows,) + split * 3,
        out_specs=(rows,) + (P("parts", None),) * 5,
        check_vma=False,
    )
```
